256 devices in a mesh: loop: 128 (over y, z, x_hi, core), grp: 2 (over x_lo).
Axes of the slice: x: 4 (x_hi: 2, x_lo: 2; x = x_hi * 2 + x_lo), y: 4, z: 8, core: 2. Of those that a mesh axis runs over, the one named last changes fastest.
Arguments:
- jacobian: float32 [768, 16384], P('grp', 'loop'), may hold values from -0.21875 to 0.21875
Outputs:
- normal_matrix: float32 [16384, 16384], P(('loop', 'grp'))
The draws below stay inside these ranges and needn't reach their ends.
All inputs are finite; a program needn't handle non-finite values.
Results may differ from the reference program's by a relative error of at most 0.00007.
Values sent between devices are 32-bit elements; how exact they have to be, the bound alone decides.
A program may use at most 128 MiB of HBM per device.

```python
import jax
import jax.numpy as jnp
from jax import lax

PARAMS = 16384
ROWS = 768


def steps_of(key, shape, cuts, low, top_value):
    level, own = 1.0, jax.random.fold_in(key, 6)
    for position, parts in cuts:
        heights = jnp.exp(jax.random.uniform(jax.random.fold_in(own, position), (parts,), jnp.float32, low / len(cuts), top_value / len(cuts)))
        level = level * jnp.repeat(heights, shape[position] // parts).reshape([-1 if axis == position else 1 for axis in range(len(shape))])
    return level


def scatter_about(stream_key, shape, scale, most, pieces=(), held_as=jnp.bfloat16):
    array = scale * jax.random.normal(stream_key, shape, jnp.float32)
    if pieces:
        array = array * steps_of(stream_key, shape, pieces, -0.22, 0.18)
    return jnp.clip(array, -most, most).astype(held_as)


def setup_inputs(seed: int = 0) -> dict:
    key_list = jax.random.split(jax.random.key(seed), 2)
    jacobian = scatter_about(key_list[0], (ROWS, PARAMS), ROWS ** -0.5, 0.21875, ((0, 2), (1, 128)), jnp.float32)
    return {"jacobian": jacobian}


damping = 0.1


def reference(jacobian):
    gram = jnp.dot(jacobian.T, jacobian, precision=lax.Precision.HIGHEST, preferred_element_type=jnp.float32)
    diag_index = jnp.arange(gram.shape[0], dtype=jnp.int32)
    return gram.at[diag_index, diag_index].multiply(1.0 + damping)
```

```python
import jax
import jax.numpy as jnp
from jax import lax
from jax.experimental import pallas as pl
from jax.experimental.pallas import tpu as pltpu
from jax.sharding import PartitionSpec as P

damping = 0.1
MESH = pl.DeviceIdType.MESH
NX, NY, NZ, NC = 4, 4, 8, 2
DEPTH, WIDTH, OWN = 384, 128, 64
FIRST = 192


def kernel(
    a_ref,
    out_ref,
    turned,
    rows_f32,
    rows_high,
    rows_low,
    cols,
    prod,
    swap_s,
    swap_r,
    row_s,
    row_r,
    pass_s,
    pass_r,
    xf_s,
    xf_r,
    zl_s,
    zl_r,
    zs_s,
    zs_r,
    xb_s,
    xb_r,
    out_s,
    out_r,
):
    loop, xl = lax.axis_index("loop"), lax.axis_index("grp")
    c = loop % 2
    xh = (loop // 2) % 2
    z = (loop // 4) % NZ
    y = loop // 32
    x = xh * 2 + xl
    me = y * 2 + c
    way = 1 - 2 * c

    def device(dx=0, dy=0, dz=0, dc=0):
        xx, yy, zz, cc = (x + dx) % NX, (y + dy) % NY, (z + dz + NZ) % NZ, (c + dc) % NC
        return ((yy * NZ + zz) * 2 + xx // 2) * 2 + cc, xx % 2

    mate = (loop, 1 - xl)
    sends = []

    def send(src, dst, s_sem, r_sem, to):
        copy = pltpu.make_async_remote_copy(
            src_ref=src, dst_ref=dst, send_sem=s_sem, recv_sem=r_sem, device_id=to, device_id_type=MESH
        )
        copy.start()
        sends.append(copy)

    def arrived(ref, r_sem, s_sem):
        pltpu.make_async_remote_copy(
            src_ref=ref, dst_ref=ref, send_sem=s_sem, recv_sem=r_sem, device_id=mate, device_id_type=MESH
        ).wait_recv()

    def piece(dx, zz, start=0, size=DEPTH):
        xx = (x + dx) % NX
        return cols.at[zz, xx // 2, pl.ds(pl.multiple_of((xx % 2) * DEPTH + start, 8), size), :]

    def first(dx, zz):
        return piece(dx, zz, 0, FIRST)

    def rest(dx, zz):
        return piece(dx, zz, FIRST, DEPTH - FIRST)

    half = pl.ds(pl.multiple_of(xl * DEPTH, 128), DEPTH)
    other_half = pl.ds(pl.multiple_of((1 - xl) * DEPTH, 128), DEPTH)

    own = a_ref[...]
    cols[z, xh, pl.ds(pl.multiple_of(xl * DEPTH, 8), DEPTH), :] = own
    turned[...] = own.T
    rows_f32[me, :, half] = turned[pl.ds(pl.multiple_of(xl * OWN, 8), OWN), :]

    barrier = pltpu.get_barrier_semaphore()
    greeted = [device(dx=d) for d in (1, 2, 3)] + [device(dz=1), device(dz=-1), device(dc=1)]
    greeted += [device(dy=d, dc=e) for d in (1, 2, 3) for e in (0, 1)]
    for who in greeted:
        pl.semaphore_signal(barrier, inc=1, device_id=who, device_id_type=MESH)
    pl.semaphore_wait(barrier, len(greeted))

    send(
        turned.at[pl.ds(pl.multiple_of((1 - xl) * OWN, 8), OWN), :],
        rows_f32.at[me, :, half],
        swap_s.at[0],
        swap_r.at[0],
        mate,
    )
    up, down = device(dz=way), device(dz=-way)
    for t in (1, 3, 2):
        send(piece(0, z), piece(0, z), xf_s.at[4 - t - 1], xf_r.at[4 - t - 1], device(dx=t))
    send(piece(0, z), piece(0, z), zl_s.at[0, 0], zl_r.at[0, 0], up)
    send(piece(0, z), piece(0, z), zs_s.at[0, 0], zs_r.at[0, 0], down)

    arrived(rows_f32.at[me, :, other_half], swap_r.at[0], swap_s.at[0])
    for t in (1, 3, 2):
        send(rows_f32.at[me], rows_f32.at[me], row_s.at[4 - t - 1], row_r.at[4 - t - 1], device(dy=t))
    send(rows_f32.at[me], rows_f32.at[me], row_s.at[3], row_r.at[3], device(dc=1))

    for dx in (1, 3, 2):
        arrived(piece(dx, z), xf_r.at[dx - 1], xf_s.at[dx - 1])
        send(first(dx, z), first(dx, z), zl_s.at[0, dx], zl_r.at[0, dx], up)
        send(first(dx, z), first(dx, z), zs_s.at[0, dx], zs_r.at[0, dx], down)

    for dy in (1, 3, 2):
        slot = rows_f32.at[((y + dy) % NY) * 2 + c]
        arrived(slot, row_r.at[dy - 1], row_s.at[dy - 1])
        send(slot, slot, pass_s.at[dy - 1], pass_r.at[dy - 1], device(dc=1))
    arrived(rows_f32.at[y * 2 + 1 - c], row_r.at[3], row_s.at[3])
    for dy in (1, 3, 2):
        arrived(rows_f32.at[((y + dy) % NY) * 2 + 1 - c], pass_r.at[dy - 1], pass_s.at[dy - 1])

    rows = rows_f32[...].reshape(NY * NC * OWN, 2 * DEPTH)
    high = rows.astype(jnp.bfloat16)
    rows_high[...] = high
    rows_low[...] = (rows - high.astype(jnp.float32)).astype(jnp.bfloat16)

    def multiply(unit, zz):
        block = jnp.concatenate([cols[zz, 0], cols[zz, 1]], axis=1)
        block_high = block.astype(jnp.bfloat16)
        block_low = (block - block_high.astype(jnp.float32)).astype(jnp.bfloat16)
        value = jnp.dot(rows_high[...], block_high, preferred_element_type=jnp.float32)
        value += jnp.dot(rows_low[...], block_high, preferred_element_type=jnp.float32)
        value += jnp.dot(rows_high[...], block_low, preferred_element_type=jnp.float32)
        prod[unit, 0] = value[:, :WIDTH]
        prod[unit, 1] = value[:, WIDTH:]
        for dy, dc in ((1, 0), (1, 1), (3, 0), (3, 1), (2, 0), (2, 1), (0, 1)):
            to = ((y + dy) % NY) * 2 + (c + dc) % NC
            there = ((4 - dy) % 4) * 2 + dc - 1
            send(
                prod.at[unit, :, pl.ds(pl.multiple_of(to * OWN, 8), OWN), :],
                out_ref.at[y, zz, :, c],
                out_s.at[unit, there],
                out_r.at[unit, there],
                device(dy=dy, dc=dc),
            )
        mine = pl.ds(pl.multiple_of(me * OWN, 8), OWN)
        out_ref[y, zz, 0, c] = prod[unit, 0, mine, :]
        out_ref[y, zz, 1, c] = prod[unit, 1, mine, :]
        if unit == 0:
            row_ids = lax.broadcasted_iota(jnp.int32, (OWN, WIDTH), 0) + xl * OWN
            col_ids = lax.broadcasted_iota(jnp.int32, (OWN, WIDTH), 1)
            factor = jnp.where(row_ids == col_ids, jnp.float32(1.0 + damping), jnp.float32(1.0))
            out_ref[y, zz, xh, c] = prod[unit, xh, mine, :] * factor

    def spread(zz, index):
        for t in (1, 3, 2):
            send(rest(0, zz), rest(0, zz), xb_s.at[index, 4 - t - 1], xb_r.at[index, 4 - t - 1], device(dx=t))

    def spread_arrived(zz, index):
        for dx in (1, 3, 2):
            arrived(rest(dx, zz), xb_r.at[index, dx - 1], xb_s.at[index, dx - 1])

    origin = lambda d: (z + d * way + NZ) % NZ
    multiply(0, z)
    for d in range(1, 5):
        low, top = origin(-d), origin(d)
        arrived(piece(0, low), zl_r.at[d - 1, 0], zl_s.at[d - 1, 0])
        if d < 4:
            send(piece(0, low), piece(0, low), zl_s.at[d, 0], zl_r.at[d, 0], up)
        spread(low, d - 1)
        if d < 4:
            arrived(piece(0, top), zs_r.at[d - 1, 0], zs_s.at[d - 1, 0])
            if d < 3:
                send(piece(0, top), piece(0, top), zs_s.at[d, 0], zs_r.at[d, 0], down)
            spread(top, 3 + d)
        for dx in (1, 3, 2):
            arrived(first(dx, low), zl_r.at[d - 1, dx], zl_s.at[d - 1, dx])
            if d < 4:
                send(first(dx, low), first(dx, low), zl_s.at[d, dx], zl_r.at[d, dx], up)
                arrived(first(dx, top), zs_r.at[d - 1, dx], zs_s.at[d - 1, dx])
                if d < 3:
                    send(first(dx, top), first(dx, top), zs_s.at[d, dx], zs_r.at[d, dx], down)
        if d > 1:
            spread_arrived(origin(1 - d), d - 2)
            multiply(2 * d - 3, origin(1 - d))
            spread_arrived(origin(d - 1), 2 + d)
            multiply(2 * d - 2, origin(d - 1))
    spread_arrived(origin(-4), 3)
    multiply(7, origin(-4))

    for unit, d in enumerate((0, -1, 1, -2, 2, -3, 3, -4)):
        for dy, dc in ((1, 0), (1, 1), (3, 0), (3, 1), (2, 0), (2, 1), (0, 1)):
            index = dy * 2 + dc - 1
            src_c = (c + dc) % NC
            zz = (z + d * (1 - 2 * src_c) + NZ) % NZ
            arrived(out_ref.at[(y + dy) % NY, zz, :, src_c], out_r.at[unit, index], out_s.at[unit, index])
    for copy in sends:
        copy.wait_send()


def per_device(jacobian):
    dma = pltpu.SemaphoreType.DMA
    tiles = pl.pallas_call(
        kernel,
        name="gather_multiply_scatter",
        out_shape=jax.ShapeDtypeStruct((NY, NZ, 2, NC, OWN, WIDTH), jnp.float32),
        in_specs=[pl.BlockSpec(memory_space=pltpu.VMEM)],
        out_specs=pl.BlockSpec(memory_space=pltpu.VMEM),
        scratch_shapes=[
            pltpu.VMEM((WIDTH, DEPTH), jnp.float32),
            pltpu.VMEM((NY * NC, OWN, 2 * DEPTH), jnp.float32),
            pltpu.VMEM((NY * NC * OWN, 2 * DEPTH), jnp.bfloat16),
            pltpu.VMEM((NY * NC * OWN, 2 * DEPTH), jnp.bfloat16),
            pltpu.VMEM((NZ, 2, 2 * DEPTH, WIDTH), jnp.float32),
            pltpu.VMEM((NZ, 2, NY * NC * OWN, WIDTH), jnp.float32),
            dma((1,)),
            dma((1,)),
            dma((4,)),
            dma((4,)),
            dma((3,)),
            dma((3,)),
            dma((3,)),
            dma((3,)),
            dma((4, 4)),
            dma((4, 4)),
            dma((3, 4)),
            dma((3, 4)),
            dma((7, 3)),
            dma((7, 3)),
            dma((8, 7)),
            dma((8, 7)),
        ],
        compiler_params=pltpu.CompilerParams(
            collective_id=0, has_side_effects=True, vmem_limit_bytes=48 * 2**20
        ),
    )(jacobian)
    tiles = tiles.reshape(NY * NZ * 2 * NC, OWN, WIDTH)
    return jnp.transpose(tiles, (1, 0, 2)).reshape(OWN, NY * NZ * 2 * NC * WIDTH)


def solution(mesh):
    return jax.shard_map(
        per_device,
        mesh=mesh,
        in_specs=(P("grp", "loop"),),
        out_specs=P(("loop", "grp"), None),
        check_vma=False,
    )
```

```python
import jax
import jax.numpy as jnp
from jax import lax
from jax.experimental import pallas as pl
from jax.experimental.pallas import tpu as pltpu
from jax.sharding import PartitionSpec as P

damping = 0.1
MESH = pl.DeviceIdType.MESH
NX, NY, NZ, NC = 4, 4, 8, 2
DEPTH, WIDTH, OWN = 384, 128, 64
FIRST = 152


SLOT = {(1, 0): 0, (3, 0): 1, (1, 1): 2, (3, 1): 3, (2, 0): 4, (2, 1): 5, (0, 0): 6, (0, 1): 7}


def kernel(
    a_ref,
    out_ref,
    own,
    turned,
    rows_f32,
    rows_high,
    rows_low,
    cols,
    prod,
    own_sem,
    swap_s,
    swap_r,
    row_s,
    row_r,
    pass_s,
    pass_r,
    xf_s,
    xf_r,
    zl_s,
    zl_r,
    zs_s,
    zs_r,
    xb_s,
    xb_r,
    out_s,
    out_r,
):
    loop, xl = lax.axis_index("loop"), lax.axis_index("grp")
    c = loop % 2
    xh = (loop // 2) % 2
    z = (loop // 4) % NZ
    y = loop // 32
    x = xh * 2 + xl
    way = 1 - 2 * c

    def device(dx=0, dy=0, dz=0, dc=0):
        xx, yy, zz = (x + dx * way + NX) % NX, (y + dy * way + NY) % NY, (z + dz * way + NZ) % NZ
        return ((yy * NZ + zz) * 2 + xx // 2) * 2 + (c + dc) % NC, xx % 2

    sends = []

    def send(src, dst, s_sem, r_sem, to):
        copy = pltpu.make_async_remote_copy(
            src_ref=src, dst_ref=dst, send_sem=s_sem, recv_sem=r_sem, device_id=to, device_id_type=MESH
        )
        copy.start()
        sends.append(copy)

    mate = (loop, 1 - xl)

    def arrived(ref, r_sem, s_sem):
        pltpu.make_async_remote_copy(
            src_ref=ref, dst_ref=ref, send_sem=s_sem, recv_sem=r_sem, device_id=mate, device_id_type=MESH
        ).wait_recv()

    def piece(dx, zz, start=0, size=DEPTH):
        xx = (x + dx * way + NX) % NX
        return cols.at[zz, xx // 2, pl.ds(pl.multiple_of((xx % 2) * DEPTH + start, 8), size), :]

    def first(dx, zz):
        return piece(dx, zz, 0, FIRST)

    def rest(dx, zz):
        return piece(dx, zz, FIRST, DEPTH - FIRST)

    def origin(d):
        return (z + d * way + NZ) % NZ

    half = pl.ds(pl.multiple_of(xl * DEPTH, 128), DEPTH)
    other_half = pl.ds(pl.multiple_of((1 - xl) * DEPTH, 128), DEPTH)

    load = pltpu.make_async_copy(a_ref, own, own_sem)
    load.start()
    barrier = pltpu.get_barrier_semaphore()
    greeted = [device(dx=d) for d in (1, 2, 3)] + [device(dz=1), device(dz=-1), device(dc=1)]
    greeted += [device(dy=d, dc=e) for d in (1, 2, 3) for e in (0, 1)]
    for who in greeted:
        pl.semaphore_signal(barrier, inc=1, device_id=who, device_id_type=MESH)
    load.wait()
    block = own[...]
    turned[...] = block.T
    rows_f32[SLOT[0, 0], :, half] = turned[pl.ds(pl.multiple_of(xl * OWN, 8), OWN), :]
    cols[z, xh, pl.ds(pl.multiple_of(xl * DEPTH, 8), DEPTH), :] = block
    pl.semaphore_wait(barrier, len(greeted))

    send(
        turned.at[pl.ds(pl.multiple_of((1 - xl) * OWN, 8), OWN), :],
        rows_f32.at[SLOT[0, 0], :, half],
        swap_s.at[0],
        swap_r.at[0],
        mate,
    )

    def give_rows(part, lanes):
        for to, there in ((1, 3), (-1, 1)):
            send(
                rows_f32.at[SLOT[0, 0], :, lanes],
                rows_f32.at[SLOT[there, 0], :, lanes],
                row_s.at[part, there - 1],
                row_r.at[part, there - 1],
                device(dy=to),
            )

    def rows_arrived(part, lanes, dy):
        slot = rows_f32.at[SLOT[dy, 0], :, lanes]
        arrived(slot, row_r.at[part, dy - 1], row_s.at[part, dy - 1])
        if dy == 3:
            send(slot, rows_f32.at[SLOT[2, 0], :, lanes], row_s.at[part, 1], row_r.at[part, 1], device(dy=1))

    def pass_rows(dy):
        send(
            rows_f32.at[SLOT[dy, 0]],
            rows_f32.at[SLOT[(4 - dy) % 4, 1]],
            pass_s.at[(4 - dy) % 4],
            pass_r.at[(4 - dy) % 4],
            device(dc=1),
        )

    def passed(dy):
        arrived(rows_f32.at[SLOT[dy, 1]], pass_r.at[dy], pass_s.at[dy])

    give_rows(0, half)
    towards = (1 - 2 * xl) * way
    for to in (towards, -towards):
        send(piece(0, z), piece(0, z), xf_s.at[1 + to], xf_r.at[1 + to], device(dx=to))
    up, down = device(dz=1), device(dz=-1)
    send(piece(0, z), piece(0, z), zl_s.at[0, 0], zl_r.at[0, 0], up)
    send(piece(0, z), piece(0, z), zs_s.at[0, 0], zs_r.at[0, 0], down)

    arrived(rows_f32.at[SLOT[0, 0], :, other_half], swap_r.at[0], swap_s.at[0])
    give_rows(1, other_half)
    pass_rows(0)
    rows_arrived(0, half, 3)
    rows_arrived(0, half, 1)
    rows_arrived(1, other_half, 3)
    pass_rows(3)
    rows_arrived(1, other_half, 1)
    pass_rows(1)

    def ring_start(dx):
        send(first(dx, z), first(dx, z), zl_s.at[0, dx], zl_r.at[0, dx], up)
        send(first(dx, z), first(dx, z), zs_s.at[0, dx], zs_r.at[0, dx], down)

    arrived(piece(3, z), xf_r.at[2], xf_s.at[2])
    send(piece(3, z), piece(3, z), xf_s.at[1], xf_r.at[1], device(dx=1))
    ring_start(3)
    arrived(piece(1, z), xf_r.at[0], xf_s.at[0])
    ring_start(1)

    def split(slots):
        part = pl.ds(slots.start * OWN, (slots.stop - slots.start) * OWN)
        rows = rows_f32[slots].reshape((slots.stop - slots.start) * OWN, 2 * DEPTH)
        high = rows.astype(jnp.bfloat16)
        rows_high[part, :] = high
        rows_low[part, :] = (rows - high.astype(jnp.float32)).astype(jnp.bfloat16)

    def product(part, block):
        block_high = block.astype(jnp.bfloat16)
        block_low = (block - block_high.astype(jnp.float32)).astype(jnp.bfloat16)
        value = jnp.dot(rows_high[part, :], block_high, preferred_element_type=jnp.float32)
        value += jnp.dot(rows_low[part, :], block_high, preferred_element_type=jnp.float32)
        value += jnp.dot(rows_high[part, :], block_low, preferred_element_type=jnp.float32)
        return value

    def deliver(group, src, dst, who):
        for dy, dc in who:
            there = (4 - dy) % 4 if dc == 0 else dy
            index = there * 2 + dc - 1
            k = SLOT[dy, dc]
            send(src(pl.ds(k * OWN, OWN)), dst, out_s.at[group, index], out_r.at[group, index], device(dy=dy, dc=dc))

    NEAR, FAR = ((1, 0), (3, 0), (1, 1), (3, 1)), ((2, 0), (2, 1), (0, 1))
    mine = pl.ds(SLOT[0, 0] * OWN, OWN)

    def own_plane(group, hh, part, who):
        prod[0, hh, part, :] = product(part, cols[z, hh])
        deliver(group, lambda r: prod.at[0, hh, r, :], out_ref.at[y, z, hh, c], who)

    near_rows, far_rows = pl.ds(0, 4 * OWN), pl.ds(4 * OWN, 4 * OWN)
    passed(1)
    passed(3)
    split(slice(0, 4))
    own_plane(0, xh, near_rows, NEAR)
    for part, lanes in ((0, half), (1, other_half)):
        rows_arrived(part, lanes, 2)
    pass_rows(2)
    arrived(piece(2, z), xf_r.at[1], xf_s.at[1])
    ring_start(2)
    passed(0)
    own_plane(8, 1 - xh, near_rows, NEAR)
    passed(2)
    split(slice(4, 8))
    own_plane(0, xh, far_rows, FAR)
    row_ids = lax.broadcasted_iota(jnp.int32, (OWN, WIDTH), 0) + xl * OWN
    col_ids = lax.broadcasted_iota(jnp.int32, (OWN, WIDTH), 1)
    factor = jnp.where(row_ids == col_ids, jnp.float32(1.0 + damping), jnp.float32(1.0))
    out_ref[y, z, xh, c] = prod[0, xh, mine, :] * factor
    own_plane(8, 1 - xh, far_rows, FAR)
    out_ref[y, z, 1 - xh, c] = prod[0, 1 - xh, mine, :]

    def multiply(unit, zz):
        value = product(pl.ds(0, 8 * OWN), jnp.concatenate([cols[zz, 0], cols[zz, 1]], axis=1))
        prod[unit, 0] = value[:, :WIDTH]
        prod[unit, 1] = value[:, WIDTH:]
        deliver(unit, lambda r: prod.at[unit, :, r, :], out_ref.at[y, zz, :, c], NEAR + FAR)
        out_ref[y, zz, 0, c] = prod[unit, 0, mine, :]
        out_ref[y, zz, 1, c] = prod[unit, 1, mine, :]

    def spread(zz, index):
        for to, there in ((1, 3), (-1, 1)):
            send(rest(0, zz), rest(0, zz), xb_s.at[index, there - 1], xb_r.at[index, there - 1], device(dx=to))

    def spread_on(zz, index):
        arrived(rest(3, zz), xb_r.at[index, 2], xb_s.at[index, 2])
        send(rest(3, zz), rest(3, zz), xb_s.at[index, 1], xb_r.at[index, 1], device(dx=1))

    def spread_done(zz, index):
        for dx in (1, 2):
            arrived(rest(dx, zz), xb_r.at[index, dx - 1], xb_s.at[index, dx - 1])

    for d in range(1, 5):
        low, top = origin(-d), origin(d)
        arrived(piece(0, low), zl_r.at[d - 1, 0], zl_s.at[d - 1, 0])
        if d < 4:
            send(piece(0, low), piece(0, low), zl_s.at[d, 0], zl_r.at[d, 0], up)
        spread(low, d - 1)
        if d < 4:
            arrived(piece(0, top), zs_r.at[d - 1, 0], zs_s.at[d - 1, 0])
            if d < 3:
                send(piece(0, top), piece(0, top), zs_s.at[d, 0], zs_r.at[d, 0], down)
            spread(top, 3 + d)
        for dx in (3, 1, 2):
            arrived(first(dx, low), zl_r.at[d - 1, dx], zl_s.at[d - 1, dx])
            if d < 4:
                send(first(dx, low), first(dx, low), zl_s.at[d, dx], zl_r.at[d, dx], up)
                arrived(first(dx, top), zs_r.at[d - 1, dx], zs_s.at[d - 1, dx])
                if d < 3:
                    send(first(dx, top), first(dx, top), zs_s.at[d, dx], zs_r.at[d, dx], down)
        spread_on(low, d - 1)
        if d < 4:
            spread_on(top, 3 + d)
        if d > 1:
            spread_done(origin(1 - d), d - 2)
            multiply(2 * d - 3, origin(1 - d))
            spread_done(origin(d - 1), 2 + d)
            multiply(2 * d - 2, origin(d - 1))
    spread_done(origin(-4), 3)
    multiply(7, origin(-4))

    for dy, dc in NEAR + FAR:
        index = dy * 2 + dc - 1
        yy, cc = (y + dy * way + NY) % NY, (c + dc) % NC
        for group, hh in ((0, xh), (8, 1 - xh)):
            arrived(out_ref.at[yy, z, hh, cc], out_r.at[group, index], out_s.at[group, index])
        for unit, d in enumerate((-1, 1, -2, 2, -3, 3, -4)):
            zz = (z + d * (1 - 2 * cc) + NZ) % NZ
            arrived(out_ref.at[yy, zz, :, cc], out_r.at[unit + 1, index], out_s.at[unit + 1, index])
    for copy in sends:
        copy.wait_send()


def per_device(jacobian):
    dma = pltpu.SemaphoreType.DMA
    tiles = pl.pallas_call(
        kernel,
        name="gather_multiply_scatter",
        out_shape=jax.ShapeDtypeStruct((NY, NZ, 2, NC, OWN, WIDTH), jnp.float32),
        in_specs=[pl.BlockSpec(memory_space=pltpu.HBM)],
        out_specs=pl.BlockSpec(memory_space=pltpu.VMEM),
        scratch_shapes=[
            pltpu.VMEM((DEPTH, WIDTH), jnp.float32),
            pltpu.VMEM((WIDTH, DEPTH), jnp.float32),
            pltpu.VMEM((NY * NC, OWN, 2 * DEPTH), jnp.float32),
            pltpu.VMEM((NY * NC * OWN, 2 * DEPTH), jnp.bfloat16),
            pltpu.VMEM((NY * NC * OWN, 2 * DEPTH), jnp.bfloat16),
            pltpu.VMEM((NZ, 2, 2 * DEPTH, WIDTH), jnp.float32),
            pltpu.VMEM((NZ, 2, NY * NC * OWN, WIDTH), jnp.float32),
            dma,
            dma((1,)),
            dma((1,)),
            dma((2, 3)),
            dma((2, 3)),
            dma((4,)),
            dma((4,)),
            dma((3,)),
            dma((3,)),
            dma((4, 4)),
            dma((4, 4)),
            dma((3, 4)),
            dma((3, 4)),
            dma((7, 3)),
            dma((7, 3)),
            dma((9, 7)),
            dma((9, 7)),
        ],
        compiler_params=pltpu.CompilerParams(
            collective_id=0, has_side_effects=True, vmem_limit_bytes=48 * 2**20
        ),
    )(jacobian)
    tiles = tiles.reshape(NY * NZ * 2 * NC, OWN, WIDTH)
    return jnp.transpose(tiles, (1, 0, 2)).reshape(OWN, NY * NZ * 2 * NC * WIDTH)


def solution(mesh):
    return jax.shard_map(
        per_device,
        mesh=mesh,
        in_specs=(P("grp", "loop"),),
        out_specs=P(("loop", "grp"), None),
        check_vma=False,
    )
```

```python
import jax
import jax.numpy as jnp
from jax import lax
from jax.experimental import pallas as pl
from jax.experimental.pallas import tpu as pltpu
from jax.sharding import PartitionSpec as P

damping = 0.1
MESH = pl.DeviceIdType.MESH
NX, NY, NZ, NC = 4, 4, 8, 2
DEPTH, WIDTH, OWN = 384, 128, 64
FIRST = 176


SLOT = {(1, 0): 0, (3, 0): 1, (1, 1): 2, (3, 1): 3, (2, 0): 4, (2, 1): 5, (0, 0): 6, (0, 1): 7}
NEAR, FAR = ((1, 0), (3, 0), (1, 1), (3, 1)), ((2, 0), (2, 1), (0, 1))
UNITS = (-1, 1, -2, 2, -3, 3, -4)
DIRECT = (-1, 1, -2, 2)
ORDER = (
    ("swap",),
    ("rows", 0, 3),
    ("first", "across"),
    ("rows", 0, 1),
    ("up", 1, "own"),
    ("passed", 0),
    ("first", "beyond"),
    ("rows", 1, 3),
    ("rows", 1, 1),
    ("down", 1, "own"),
    ("passed", 1),
    ("first", "opposite"),
    ("rows", 0, 2),
    ("up", 1, "across"),
    ("rest", "across"),
    ("passed", 3),
    ("near", 0),
    ("rows", 1, 2),
    ("down", 1, "across"),
    ("rest", "beyond"),
    ("passed", 2),
    ("far", 0),
    ("up", 2, "own"),
    ("up", 1, "beyond"),
    ("rest", "opposite"),
    ("near", 8),
    ("spread", -1, 3),
    ("far", 8),
    ("down", 1, "beyond"),
    ("spread", -1, 1),
    ("down", 2, "own"),
    ("up", 1, "opposite"),
    ("spread", -1, 2),
    ("multiply", -1),
    ("down", 1, "opposite"),
    ("spread", 1, 3),
    ("up", 2, "across"),
    ("spread", 1, 1),
    ("down", 2, "across"),
    ("up", 3, "own"),
    ("spread", 1, 2),
    ("multiply", 1),
    ("spread", -2, 3),
    ("up", 2, "beyond"),
    ("down", 2, "beyond"),
    ("spread", -2, 1),
    ("down", 3, "own"),
    ("spread", -2, 2),
    ("up", 2, "opposite"),
    ("multiply", -2),
    ("spread", 2, 3),
    ("down", 2, "opposite"),
    ("spread", 2, 1),
    ("up", 3, "across"),
    ("down", 3, "across"),
    ("spread", 2, 2),
    ("multiply", 2),
    ("spread", -3, 3),
    ("up", 4, "own"),
    ("up", 3, "beyond"),
    ("spread", -3, 1),
    ("down", 3, "beyond"),
    ("spread", 3, 3),
    ("up", 3, "opposite"),
    ("spread", 3, 1),
    ("down", 3, "opposite"),
    ("spread", -3, 2),
    ("multiply", -3),
    ("up", 4, "across"),
    ("spread", -4, 3),
    ("up", 4, "beyond"),
    ("up", 4, "opposite"),
    ("spread", -4, 1),
    ("spread", 3, 2),
    ("multiply", 3),
    ("spread", -4, 2),
    ("multiply", -4),
)


def kernel(
    a_ref,
    out_ref,
    own,
    turned,
    rows_f32,
    rows_high,
    rows_low,
    cols,
    prod,
    own_sem,
    swap_s,
    swap_r,
    row_s,
    row_r,
    pass_s,
    pass_r,
    xa_s,
    xa_r,
    xf_s,
    xf_r,
    zl_s,
    zl_r,
    zs_s,
    zs_r,
    xb_s,
    xb_r,
    out_s,
    out_r,
):
    loop, xl = lax.axis_index("loop"), lax.axis_index("grp")
    c = loop % 2
    xh = (loop // 2) % 2
    z = (loop // 4) % NZ
    y = loop // 32
    x = xh * 2 + xl
    way = 1 - 2 * c

    def device(dx=0, dy=0, dz=0, dc=0):
        xx, yy, zz = (x + dx * way + NX) % NX, (y + dy * way + NY) % NY, (z + dz * way + NZ) % NZ
        return ((yy * NZ + zz) * 2 + xx // 2) * 2 + (c + dc) % NC, xx % 2

    sends = []

    def send(src, dst, s_sem, r_sem, to):
        copy = pltpu.make_async_remote_copy(
            src_ref=src, dst_ref=dst, send_sem=s_sem, recv_sem=r_sem, device_id=to, device_id_type=MESH
        )
        copy.start()
        sends.append(copy)

    mate = (loop, 1 - xl)

    def arrived(ref, r_sem, s_sem):
        pltpu.make_async_remote_copy(
            src_ref=ref, dst_ref=ref, send_sem=s_sem, recv_sem=r_sem, device_id=mate, device_id_type=MESH
        ).wait_recv()

    def piece(dx, zz, start=0, size=DEPTH):
        xx = (x + dx * way + NX) % NX
        return cols.at[zz, xx // 2, pl.ds(pl.multiple_of((xx % 2) * DEPTH + start, 8), size), :]

    def first(dx, zz):
        return piece(dx, zz, 0, FIRST)

    def rest(dx, zz):
        return piece(dx, zz, FIRST, DEPTH - FIRST)

    def origin(d):
        return (z + d * way + NZ) % NZ

    half = pl.ds(pl.multiple_of(xl * DEPTH, 128), DEPTH)
    other_half = pl.ds(pl.multiple_of((1 - xl) * DEPTH, 128), DEPTH)

    load = pltpu.make_async_copy(a_ref, own, own_sem)
    load.start()
    barrier = pltpu.get_barrier_semaphore()
    greeted = [device(dx=d) for d in (1, 2, 3)] + [device(dz=1), device(dz=-1), device(dc=1)]
    greeted += [device(dy=d, dc=e) for d in (1, 2, 3) for e in (0, 1)]
    for who in greeted:
        pl.semaphore_signal(barrier, inc=1, device_id=who, device_id_type=MESH)
    load.wait()
    block = own[...]
    turned[...] = block.T
    rows_f32[SLOT[0, 0], :, half] = turned[pl.ds(pl.multiple_of(xl * OWN, 8), OWN), :]
    cols[z, xh, pl.ds(pl.multiple_of(xl * DEPTH, 8), DEPTH), :] = block
    pl.semaphore_wait(barrier, len(greeted))

    send(
        turned.at[pl.ds(pl.multiple_of((1 - xl) * OWN, 8), OWN), :],
        rows_f32.at[SLOT[0, 0], :, half],
        swap_s.at[0],
        swap_r.at[0],
        mate,
    )

    def give_rows(part, lanes):
        for to, there in ((1, 3), (-1, 1)):
            send(
                rows_f32.at[SLOT[0, 0], :, lanes],
                rows_f32.at[SLOT[there, 0], :, lanes],
                row_s.at[part, there - 1],
                row_r.at[part, there - 1],
                device(dy=to),
            )

    def rows_arrived(part, lanes, dy):
        slot = rows_f32.at[SLOT[dy, 0], :, lanes]
        arrived(slot, row_r.at[part, dy - 1], row_s.at[part, dy - 1])
        if dy == 3:
            send(slot, rows_f32.at[SLOT[2, 0], :, lanes], row_s.at[part, 1], row_r.at[part, 1], device(dy=1))

    def pass_rows(dy):
        send(
            rows_f32.at[SLOT[dy, 0]],
            rows_f32.at[SLOT[(4 - dy) % 4, 1]],
            pass_s.at[(4 - dy) % 4],
            pass_r.at[(4 - dy) % 4],
            device(dc=1),
        )

    def passed(dy):
        arrived(rows_f32.at[SLOT[dy, 1]], pass_r.at[dy], pass_s.at[dy])

    towards = (1 - 2 * xl) * way
    across, beyond = (towards + NX) % NX, (NX - towards) % NX
    up, down = device(dz=1), device(dz=-1)
    near_rows, far_rows = pl.ds(0, 4 * OWN), pl.ds(4 * OWN, 4 * OWN)
    mine = pl.ds(SLOT[0, 0] * OWN, OWN)

    def split(slots):
        part = pl.ds(slots.start * OWN, (slots.stop - slots.start) * OWN)
        rows = rows_f32[slots].reshape((slots.stop - slots.start) * OWN, 2 * DEPTH)
        high = rows.astype(jnp.bfloat16)
        rows_high[part, :] = high
        rows_low[part, :] = (rows - high.astype(jnp.float32)).astype(jnp.bfloat16)

    def product(part, block):
        block_high = block.astype(jnp.bfloat16)
        block_low = (block - block_high.astype(jnp.float32)).astype(jnp.bfloat16)
        value = jnp.dot(rows_high[part, :], block_high, preferred_element_type=jnp.float32)
        value += jnp.dot(rows_low[part, :], block_high, preferred_element_type=jnp.float32)
        value += jnp.dot(rows_high[part, :], block_low, preferred_element_type=jnp.float32)
        return value

    def deliver(group, src, dst, who):
        for dy, dc in who:
            there = (4 - dy) % 4 if dc == 0 else dy
            index = there * 2 + dc - 1
            k = SLOT[dy, dc]
            send(src(pl.ds(k * OWN, OWN)), dst, out_s.at[group, index], out_r.at[group, index], device(dy=dy, dc=dc))

    def own_plane(group, hh, part, who):
        prod[0, hh, part, :] = product(part, cols[z, hh])
        deliver(group, lambda r: prod.at[0, hh, r, :], out_ref.at[y, z, hh, c], who)

    def plane_near(group, hh):
        if group == 0:
            split(slice(0, 4))
        own_plane(group, hh, near_rows, NEAR)

    def plane_far(group, hh):
        if group == 0:
            split(slice(4, 8))
        own_plane(group, hh, far_rows, FAR)
        if group == 0:
            row_ids = lax.broadcasted_iota(jnp.int32, (OWN, WIDTH), 0) + xl * OWN
            col_ids = lax.broadcasted_iota(jnp.int32, (OWN, WIDTH), 1)
            factor = jnp.where(row_ids == col_ids, jnp.float32(1.0 + damping), jnp.float32(1.0))
            out_ref[y, z, hh, c] = prod[0, hh, mine, :] * factor
        else:
            out_ref[y, z, hh, c] = prod[0, hh, mine, :]

    def multiply(d):
        unit, zz = UNITS.index(d) + 1, origin(d)
        value = product(pl.ds(0, 8 * OWN), jnp.concatenate([cols[zz, 0], cols[zz, 1]], axis=1))
        prod[unit, 0] = value[:, :WIDTH]
        prod[unit, 1] = value[:, WIDTH:]
        deliver(unit, lambda r: prod.at[unit, :, r, :], out_ref.at[y, zz, :, c], NEAR + FAR)
        out_ref[y, zz, 0, c] = prod[unit, 0, mine, :]
        out_ref[y, zz, 1, c] = prod[unit, 1, mine, :]

    def ring_start(dx, part):
        send(part, part, zl_s.at[0, dx], zl_r.at[0, dx], up)
        send(part, part, zs_s.at[0, dx], zs_r.at[0, dx], down)

    def ring_up(d, dx):
        part = piece(0, origin(-d)) if isinstance(dx, int) and dx == 0 else first(dx, origin(-d))
        arrived(part, zl_r.at[d - 1, dx], zl_s.at[d - 1, dx])
        if d < 4:
            send(part, part, zl_s.at[d, dx], zl_r.at[d, dx], up)

    def ring_down(d, dx):
        part = piece(0, origin(d)) if isinstance(dx, int) and dx == 0 else first(dx, origin(d))
        arrived(part, zs_r.at[d - 1, dx], zs_s.at[d - 1, dx])
        if d < 3:
            send(part, part, zs_s.at[d, dx], zs_r.at[d, dx], down)

    def spread(d):
        part, unit = rest(0, origin(d)), UNITS.index(d)
        for to, there in ((1, 3), (-1, 1)):
            send(part, part, xb_s.at[unit, there - 1], xb_r.at[unit, there - 1], device(dx=to))
        if d in DIRECT:
            send(part, part, xb_s.at[unit, 1], xb_r.at[unit, 1], device(dx=2))

    def spread_came(d, dx):
        part, unit = rest(dx, origin(d)), UNITS.index(d)
        arrived(part, xb_r.at[unit, dx - 1], xb_s.at[unit, dx - 1])
        if dx == 3 and d not in DIRECT:
            send(part, part, xb_s.at[unit, 1], xb_r.at[unit, 1], device(dx=1))

    give_rows(0, half)
    for part, s_sem, r_sem in ((first(0, z), xa_s, xa_r), (rest(0, z), xf_s, xf_r)):
        send(part, part, s_sem.at[1 + towards], r_sem.at[1 + towards], device(dx=towards))
        if s_sem is xa_s:
            ring_start(0, piece(0, z))
        send(part, part, s_sem.at[1 - towards], r_sem.at[1 - towards], device(dx=-towards))
        send(part, part, s_sem.at[1], r_sem.at[1], device(dx=2))

    for event in ORDER:
        kind, at = event[0], event[1:]
        if kind == "swap":
            arrived(rows_f32.at[SLOT[0, 0], :, other_half], swap_r.at[0], swap_s.at[0])
            give_rows(1, other_half)
            pass_rows(0)
        elif kind == "rows":
            rows_arrived(at[0], (half, other_half)[at[0]], at[1])
            if at[0] == 1:
                pass_rows(at[1])
        elif kind == "passed":
            passed(at[0])
        elif kind in ("first", "rest"):
            dx = {"across": across, "beyond": beyond, "opposite": 2}[at[0]]
            if kind == "first":
                arrived(first(dx, z), xa_r.at[dx - 1], xa_s.at[dx - 1])
                ring_start(dx, first(dx, z))
            else:
                arrived(rest(dx, z), xf_r.at[dx - 1], xf_s.at[dx - 1])
        elif kind in ("up", "down"):
            dx = {"own": 0, "across": across, "beyond": beyond, "opposite": 2}[at[1]]
            (ring_up if kind == "up" else ring_down)(at[0], dx)
            if at[1] == "own":
                spread(-at[0] if kind == "up" else at[0])
        elif kind == "spread":
            spread_came(at[0], at[1])
        elif kind == "near":
            plane_near(at[0], xh if at[0] == 0 else 1 - xh)
        elif kind == "far":
            plane_far(at[0], xh if at[0] == 0 else 1 - xh)
        else:
            multiply(at[0])

    for dy, dc in NEAR + FAR:
        index = dy * 2 + dc - 1
        yy, cc = (y + dy * way + NY) % NY, (c + dc) % NC
        for group, hh in ((0, xh), (8, 1 - xh)):
            arrived(out_ref.at[yy, z, hh, cc], out_r.at[group, index], out_s.at[group, index])
        for unit, d in enumerate(UNITS):
            zz = (z + d * (1 - 2 * cc) + NZ) % NZ
            arrived(out_ref.at[yy, zz, :, cc], out_r.at[unit + 1, index], out_s.at[unit + 1, index])
    for copy in sends:
        copy.wait_send()


def per_device(jacobian):
    dma = pltpu.SemaphoreType.DMA
    tiles = pl.pallas_call(
        kernel,
        name="gather_multiply_scatter",
        out_shape=jax.ShapeDtypeStruct((NY, NZ, 2, NC, OWN, WIDTH), jnp.float32),
        in_specs=[pl.BlockSpec(memory_space=pltpu.HBM)],
        out_specs=pl.BlockSpec(memory_space=pltpu.VMEM),
        scratch_shapes=[
            pltpu.VMEM((DEPTH, WIDTH), jnp.float32),
            pltpu.VMEM((WIDTH, DEPTH), jnp.float32),
            pltpu.VMEM((NY * NC, OWN, 2 * DEPTH), jnp.float32),
            pltpu.VMEM((NY * NC * OWN, 2 * DEPTH), jnp.bfloat16),
            pltpu.VMEM((NY * NC * OWN, 2 * DEPTH), jnp.bfloat16),
            pltpu.VMEM((NZ, 2, 2 * DEPTH, WIDTH), jnp.float32),
            pltpu.VMEM((NZ, 2, NY * NC * OWN, WIDTH), jnp.float32),
            dma,
            dma((1,)),
            dma((1,)),
            dma((2, 3)),
            dma((2, 3)),
            dma((4,)),
            dma((4,)),
            dma((3,)),
            dma((3,)),
            dma((3,)),
            dma((3,)),
            dma((4, 4)),
            dma((4, 4)),
            dma((3, 4)),
            dma((3, 4)),
            dma((7, 3)),
            dma((7, 3)),
            dma((9, 7)),
            dma((9, 7)),
        ],
        compiler_params=pltpu.CompilerParams(
            collective_id=0, has_side_effects=True, vmem_limit_bytes=48 * 2**20
        ),
    )(jacobian)
    tiles = tiles.reshape(NY * NZ * 2 * NC, OWN, WIDTH)
    return jnp.transpose(tiles, (1, 0, 2)).reshape(OWN, NY * NZ * 2 * NC * WIDTH)


def solution(mesh):
    return jax.shard_map(
        per_device,
        mesh=mesh,
        in_specs=(P("grp", "loop"),),
        out_specs=P(("loop", "grp"), None),
        check_vma=False,
    )
```

```python
import jax
import jax.numpy as jnp
from jax import lax
from jax.experimental import pallas as pl
from jax.experimental.pallas import tpu as pltpu
from jax.sharding import PartitionSpec as P

damping = 0.1
MESH = pl.DeviceIdType.MESH
NX, NY, NZ, NC = 4, 4, 8, 2
DEPTH, WIDTH, OWN = 384, 128, 64
TILES = OWN // 8
FIRST = 176


SLOT = {(1, 0): 0, (3, 0): 1, (1, 1): 2, (3, 1): 3, (2, 0): 4, (2, 1): 5, (0, 0): 6, (0, 1): 7}
NEAR, FAR = ((1, 0), (3, 0), (1, 1), (3, 1)), ((2, 0), (2, 1), (0, 1))
UNITS = (-1, 1, -2, 2, -3, 3, -4)
DIRECT = (-1, 1, -2, 2)
ORDER = (
    ("swap",),
    ("rows", 0, 3),
    ("first", "across"),
    ("rows", 0, 1),
    ("up", 1, "own"),
    ("passed", 0),
    ("first", "beyond"),
    ("rows", 1, 3),
    ("rows", 1, 1),
    ("down", 1, "own"),
    ("passed", 1),
    ("first", "opposite"),
    ("rows", 0, 2),
    ("up", 1, "across"),
    ("rest", "across"),
    ("passed", 3),
    ("near", 0),
    ("rows", 1, 2),
    ("down", 1, "across"),
    ("rest", "beyond"),
    ("passed", 2),
    ("far", 0),
    ("up", 2, "own"),
    ("up", 1, "beyond"),
    ("rest", "opposite"),
    ("near", 8),
    ("spread", -1, 3),
    ("far", 8),
    ("down", 1, "beyond"),
    ("spread", -1, 1),
    ("down", 2, "own"),
    ("up", 1, "opposite"),
    ("spread", -1, 2),
    ("multiply", -1),
    ("down", 1, "opposite"),
    ("spread", 1, 3),
    ("up", 2, "across"),
    ("spread", 1, 1),
    ("down", 2, "across"),
    ("up", 3, "own"),
    ("spread", 1, 2),
    ("multiply", 1),
    ("spread", -2, 3),
    ("up", 2, "beyond"),
    ("down", 2, "beyond"),
    ("spread", -2, 1),
    ("down", 3, "own"),
    ("spread", -2, 2),
    ("up", 2, "opposite"),
    ("multiply", -2),
    ("spread", 2, 3),
    ("down", 2, "opposite"),
    ("spread", 2, 1),
    ("up", 3, "across"),
    ("down", 3, "across"),
    ("spread", 2, 2),
    ("multiply", 2),
    ("spread", -3, 3),
    ("up", 4, "own"),
    ("up", 3, "beyond"),
    ("spread", -3, 1),
    ("down", 3, "beyond"),
    ("spread", 3, 3),
    ("up", 3, "opposite"),
    ("spread", 3, 1),
    ("down", 3, "opposite"),
    ("spread", -3, 2),
    ("multiply", -3),
    ("up", 4, "across"),
    ("spread", -4, 3),
    ("up", 4, "beyond"),
    ("up", 4, "opposite"),
    ("spread", -4, 1),
    ("spread", 3, 2),
    ("multiply", 3),
    ("spread", -4, 2),
    ("multiply", -4),
)


def kernel(
    a_ref,
    out_ref,
    own,
    turned,
    rows_f32,
    rows_high,
    rows_low,
    cols,
    prod,
    own_sem,
    swap_s,
    swap_r,
    row_s,
    row_r,
    pass_s,
    pass_r,
    xa_s,
    xa_r,
    xf_s,
    xf_r,
    zl_s,
    zl_r,
    zs_s,
    zs_r,
    xb_s,
    xb_r,
    out_s,
    out_r,
):
    loop, xl = lax.axis_index("loop"), lax.axis_index("grp")
    c = loop % 2
    xh = (loop // 2) % 2
    z = (loop // 4) % NZ
    y = loop // 32
    x = xh * 2 + xl
    way = 1 - 2 * c

    def device(dx=0, dy=0, dz=0, dc=0):
        xx, yy, zz = (x + dx * way + NX) % NX, (y + dy * way + NY) % NY, (z + dz * way + NZ) % NZ
        return ((yy * NZ + zz) * 2 + xx // 2) * 2 + (c + dc) % NC, xx % 2

    sends = []

    def send(src, dst, s_sem, r_sem, to):
        copy = pltpu.make_async_remote_copy(
            src_ref=src, dst_ref=dst, send_sem=s_sem, recv_sem=r_sem, device_id=to, device_id_type=MESH
        )
        copy.start()
        sends.append(copy)

    mate = (loop, 1 - xl)

    def arrived(ref, r_sem, s_sem):
        pltpu.make_async_remote_copy(
            src_ref=ref, dst_ref=ref, send_sem=s_sem, recv_sem=r_sem, device_id=mate, device_id_type=MESH
        ).wait_recv()

    def piece(dx, zz, start=0, size=DEPTH):
        xx = (x + dx * way + NX) % NX
        return cols.at[zz, xx // 2, pl.ds(pl.multiple_of((xx % 2) * DEPTH + start, 8), size), :]

    def first(dx, zz):
        return piece(dx, zz, 0, FIRST)

    def rest(dx, zz):
        return piece(dx, zz, FIRST, DEPTH - FIRST)

    def origin(d):
        return (z + d * way + NZ) % NZ

    half = pl.ds(pl.multiple_of(xl * DEPTH, 128), DEPTH)
    other_half = pl.ds(pl.multiple_of((1 - xl) * DEPTH, 128), DEPTH)

    load = pltpu.make_async_copy(a_ref, own, own_sem)
    load.start()
    barrier = pltpu.get_barrier_semaphore()
    greeted = [device(dx=d) for d in (1, 2, 3)] + [device(dz=1), device(dz=-1), device(dc=1)]
    greeted += [device(dy=d, dc=e) for d in (1, 2, 3) for e in (0, 1)]
    for who in greeted:
        pl.semaphore_signal(barrier, inc=1, device_id=who, device_id_type=MESH)
    load.wait()
    block = own[...]
    turned[...] = block.T
    rows_f32[SLOT[0, 0], :, half] = turned[pl.ds(pl.multiple_of(xl * OWN, 8), OWN), :]
    cols[z, xh, pl.ds(pl.multiple_of(xl * DEPTH, 8), DEPTH), :] = block
    pl.semaphore_wait(barrier, len(greeted))

    send(
        turned.at[pl.ds(pl.multiple_of((1 - xl) * OWN, 8), OWN), :],
        rows_f32.at[SLOT[0, 0], :, half],
        swap_s.at[0],
        swap_r.at[0],
        mate,
    )

    def give_rows(part, lanes):
        for to, there in ((1, 3), (-1, 1)):
            send(
                rows_f32.at[SLOT[0, 0], :, lanes],
                rows_f32.at[SLOT[there, 0], :, lanes],
                row_s.at[part, there - 1],
                row_r.at[part, there - 1],
                device(dy=to),
            )

    def rows_arrived(part, lanes, dy):
        slot = rows_f32.at[SLOT[dy, 0], :, lanes]
        arrived(slot, row_r.at[part, dy - 1], row_s.at[part, dy - 1])
        if dy == 3:
            send(slot, rows_f32.at[SLOT[2, 0], :, lanes], row_s.at[part, 1], row_r.at[part, 1], device(dy=1))

    def pass_rows(dy):
        send(
            rows_f32.at[SLOT[dy, 0]],
            rows_f32.at[SLOT[(4 - dy) % 4, 1]],
            pass_s.at[(4 - dy) % 4],
            pass_r.at[(4 - dy) % 4],
            device(dc=1),
        )

    def passed(dy):
        arrived(rows_f32.at[SLOT[dy, 1]], pass_r.at[dy], pass_s.at[dy])

    towards = (1 - 2 * xl) * way
    across, beyond = (towards + NX) % NX, (NX - towards) % NX
    up, down = device(dz=1), device(dz=-1)
    near_rows, far_rows = pl.ds(0, 4 * OWN), pl.ds(4 * OWN, 4 * OWN)
    mine = pl.ds(SLOT[0, 0] * TILES, TILES)

    def part_tiles(part):
        return pl.ds(part.start // 8, part.size // 8)

    def tiles_of(value):
        return value.reshape(value.shape[0] // 8, 8, WIDTH)


    def split(slots):
        part = pl.ds(slots.start * OWN, (slots.stop - slots.start) * OWN)
        rows = rows_f32[slots].reshape((slots.stop - slots.start) * OWN, 2 * DEPTH)
        high = rows.astype(jnp.bfloat16)
        rows_high[part, :] = high
        rows_low[part, :] = (rows - high.astype(jnp.float32)).astype(jnp.bfloat16)

    def product(part, block):
        block_high = block.astype(jnp.bfloat16)
        block_low = (block - block_high.astype(jnp.float32)).astype(jnp.bfloat16)
        value = jnp.dot(rows_high[part, :], block_high, preferred_element_type=jnp.float32)
        value += jnp.dot(rows_low[part, :], block_high, preferred_element_type=jnp.float32)
        value += jnp.dot(rows_high[part, :], block_low, preferred_element_type=jnp.float32)
        return value

    def deliver(group, src, dst, who):
        for dy, dc in who:
            there = (4 - dy) % 4 if dc == 0 else dy
            index = there * 2 + dc - 1
            k = SLOT[dy, dc]
            send(src(pl.ds(k * TILES, TILES)), dst, out_s.at[group, index], out_r.at[group, index], device(dy=dy, dc=dc))

    def own_plane(group, hh, part, who):
        prod[0, part_tiles(part), hh] = tiles_of(product(part, cols[z, hh]))
        deliver(group, lambda t: prod.at[0, t, hh], out_ref.at[:, y, z, hh, c], who)

    def plane_near(group, hh):
        if group == 0:
            split(slice(0, 4))
        own_plane(group, hh, near_rows, NEAR)

    def plane_far(group, hh):
        if group == 0:
            split(slice(4, 8))
        own_plane(group, hh, far_rows, FAR)
        if group == 0:
            row_ids = lax.broadcasted_iota(jnp.int32, (TILES, 8, WIDTH), 0) * 8 + xl * OWN
            row_ids += lax.broadcasted_iota(jnp.int32, (TILES, 8, WIDTH), 1)
            col_ids = lax.broadcasted_iota(jnp.int32, (TILES, 8, WIDTH), 2)
            factor = jnp.where(row_ids == col_ids, jnp.float32(1.0 + damping), jnp.float32(1.0))
            out_ref[:, y, z, hh, c] = prod[0, mine, hh] * factor
        else:
            out_ref[:, y, z, hh, c] = prod[0, mine, hh]

    def multiply(d):
        unit, zz = UNITS.index(d) + 1, origin(d)
        value = product(pl.ds(0, 8 * OWN), jnp.concatenate([cols[zz, 0], cols[zz, 1]], axis=1))
        prod[unit, :, 0] = tiles_of(value[:, :WIDTH])
        prod[unit, :, 1] = tiles_of(value[:, WIDTH:])
        deliver(unit, lambda t: prod.at[unit, t], out_ref.at[:, y, zz, :, c], NEAR + FAR)
        out_ref[:, y, zz, 0, c] = prod[unit, mine, 0]
        out_ref[:, y, zz, 1, c] = prod[unit, mine, 1]

    def ring_start(dx, part):
        send(part, part, zl_s.at[0, dx], zl_r.at[0, dx], up)
        send(part, part, zs_s.at[0, dx], zs_r.at[0, dx], down)

    def ring_up(d, dx):
        part = piece(0, origin(-d)) if isinstance(dx, int) and dx == 0 else first(dx, origin(-d))
        arrived(part, zl_r.at[d - 1, dx], zl_s.at[d - 1, dx])
        if d < 4:
            send(part, part, zl_s.at[d, dx], zl_r.at[d, dx], up)

    def ring_down(d, dx):
        part = piece(0, origin(d)) if isinstance(dx, int) and dx == 0 else first(dx, origin(d))
        arrived(part, zs_r.at[d - 1, dx], zs_s.at[d - 1, dx])
        if d < 3:
            send(part, part, zs_s.at[d, dx], zs_r.at[d, dx], down)

    def spread(d):
        part, unit = rest(0, origin(d)), UNITS.index(d)
        for to, there in ((1, 3), (-1, 1)):
            send(part, part, xb_s.at[unit, there - 1], xb_r.at[unit, there - 1], device(dx=to))
        if d in DIRECT:
            send(part, part, xb_s.at[unit, 1], xb_r.at[unit, 1], device(dx=2))

    def spread_came(d, dx):
        part, unit = rest(dx, origin(d)), UNITS.index(d)
        arrived(part, xb_r.at[unit, dx - 1], xb_s.at[unit, dx - 1])
        if dx == 3 and d not in DIRECT:
            send(part, part, xb_s.at[unit, 1], xb_r.at[unit, 1], device(dx=1))

    give_rows(0, half)
    for part, s_sem, r_sem in ((first(0, z), xa_s, xa_r), (rest(0, z), xf_s, xf_r)):
        send(part, part, s_sem.at[1 + towards], r_sem.at[1 + towards], device(dx=towards))
        if s_sem is xa_s:
            ring_start(0, piece(0, z))
        send(part, part, s_sem.at[1 - towards], r_sem.at[1 - towards], device(dx=-towards))
        send(part, part, s_sem.at[1], r_sem.at[1], device(dx=2))

    for event in ORDER:
        kind, at = event[0], event[1:]
        if kind == "swap":
            arrived(rows_f32.at[SLOT[0, 0], :, other_half], swap_r.at[0], swap_s.at[0])
            give_rows(1, other_half)
            pass_rows(0)
        elif kind == "rows":
            rows_arrived(at[0], (half, other_half)[at[0]], at[1])
            if at[0] == 1:
                pass_rows(at[1])
        elif kind == "passed":
            passed(at[0])
        elif kind in ("first", "rest"):
            dx = {"across": across, "beyond": beyond, "opposite": 2}[at[0]]
            if kind == "first":
                arrived(first(dx, z), xa_r.at[dx - 1], xa_s.at[dx - 1])
                ring_start(dx, first(dx, z))
            else:
                arrived(rest(dx, z), xf_r.at[dx - 1], xf_s.at[dx - 1])
        elif kind in ("up", "down"):
            dx = {"own": 0, "across": across, "beyond": beyond, "opposite": 2}[at[1]]
            (ring_up if kind == "up" else ring_down)(at[0], dx)
            if at[1] == "own":
                spread(-at[0] if kind == "up" else at[0])
        elif kind == "spread":
            spread_came(at[0], at[1])
        elif kind == "near":
            plane_near(at[0], xh if at[0] == 0 else 1 - xh)
        elif kind == "far":
            plane_far(at[0], xh if at[0] == 0 else 1 - xh)
        else:
            multiply(at[0])

    for dy, dc in NEAR + FAR:
        index = dy * 2 + dc - 1
        yy, cc = (y + dy * way + NY) % NY, (c + dc) % NC
        for group, hh in ((0, xh), (8, 1 - xh)):
            arrived(out_ref.at[:, yy, z, hh, cc], out_r.at[group, index], out_s.at[group, index])
        for unit, d in enumerate(UNITS):
            zz = (z + d * (1 - 2 * cc) + NZ) % NZ
            arrived(out_ref.at[:, yy, zz, :, cc], out_r.at[unit + 1, index], out_s.at[unit + 1, index])
    for copy in sends:
        copy.wait_send()


def per_device(jacobian):
    dma = pltpu.SemaphoreType.DMA
    tiles = pl.pallas_call(
        kernel,
        name="gather_multiply_scatter",
        out_shape=jax.ShapeDtypeStruct((TILES, NY, NZ, 2, NC, 8, WIDTH), jnp.float32),
        in_specs=[pl.BlockSpec(memory_space=pltpu.HBM)],
        out_specs=pl.BlockSpec(memory_space=pltpu.VMEM),
        scratch_shapes=[
            pltpu.VMEM((DEPTH, WIDTH), jnp.float32),
            pltpu.VMEM((WIDTH, DEPTH), jnp.float32),
            pltpu.VMEM((NY * NC, OWN, 2 * DEPTH), jnp.float32),
            pltpu.VMEM((NY * NC * OWN, 2 * DEPTH), jnp.bfloat16),
            pltpu.VMEM((NY * NC * OWN, 2 * DEPTH), jnp.bfloat16),
            pltpu.VMEM((NZ, 2, 2 * DEPTH, WIDTH), jnp.float32),
            pltpu.VMEM((NZ, NY * NC * TILES, 2, 8, WIDTH), jnp.float32),
            dma,
            dma((1,)),
            dma((1,)),
            dma((2, 3)),
            dma((2, 3)),
            dma((4,)),
            dma((4,)),
            dma((3,)),
            dma((3,)),
            dma((3,)),
            dma((3,)),
            dma((4, 4)),
            dma((4, 4)),
            dma((3, 4)),
            dma((3, 4)),
            dma((7, 3)),
            dma((7, 3)),
            dma((9, 7)),
            dma((9, 7)),
        ],
        compiler_params=pltpu.CompilerParams(
            collective_id=0, has_side_effects=True, vmem_limit_bytes=48 * 2**20
        ),
    )(pltpu.with_memory_space_constraint(jacobian, pltpu.HBM))
    tiles = tiles.reshape(TILES, NY * NZ * 2 * NC, 8, WIDTH)
    return jnp.transpose(tiles, (0, 2, 1, 3)).reshape(OWN, NY * NZ * 2 * NC * WIDTH)


def solution(mesh):
    return jax.shard_map(
        per_device,
        mesh=mesh,
        in_specs=(P("grp", "loop"),),
        out_specs=P(("loop", "grp"), None),
        check_vma=False,
    )
```

```python
import jax
import jax.numpy as jnp
from jax import lax
from jax.experimental import pallas as pl
from jax.experimental.pallas import tpu as pltpu
from jax.sharding import PartitionSpec as P

damping = 0.1
MESH = pl.DeviceIdType.MESH
NX, NY, NZ, NC = 4, 4, 8, 2
DEPTH, WIDTH, OWN = 384, 128, 64
TILES = OWN // 8
FIRST = 176


SLOT = {(1, 0): 0, (3, 0): 1, (1, 1): 2, (3, 1): 3, (2, 0): 4, (2, 1): 5, (0, 0): 6, (0, 1): 7}
NEAR, FAR = ((1, 0), (3, 0), (1, 1), (3, 1)), ((2, 0), (2, 1), (0, 1))
UNITS = (-1, 1, -2, 2, -3, 3, -4)
MIRRORED = (-1, 1)
DIRECT = (-1, 1, -2, 2)
ORDER = (
    ("swap",),
    ("rows", 0, 3),
    ("first", "across"),
    ("rows", 0, 1),
    ("up", 1, "own"),
    ("passed", 0),
    ("first", "beyond"),
    ("rows", 1, 3),
    ("rows", 1, 1),
    ("down", 1, "own"),
    ("passed", 1),
    ("first", "opposite"),
    ("rows", 0, 2),
    ("up", 1, "across"),
    ("rest", "across"),
    ("passed", 3),
    ("near", 0),
    ("rows", 1, 2),
    ("down", 1, "across"),
    ("rest", "beyond"),
    ("passed", 2),
    ("far", 0),
    ("up", 2, "own"),
    ("up", 1, "beyond"),
    ("rest", "opposite"),
    ("near", 8),
    ("spread", -1, 3),
    ("far", 8),
    ("down", 1, "beyond"),
    ("spread", -1, 1),
    ("down", 2, "own"),
    ("up", 1, "opposite"),
    ("spread", -1, 2),
    ("multiply", -1),
    ("down", 1, "opposite"),
    ("spread", 1, 3),
    ("up", 2, "across"),
    ("spread", 1, 1),
    ("down", 2, "across"),
    ("up", 3, "own"),
    ("spread", 1, 2),
    ("multiply", 1),
    ("spread", -2, 3),
    ("up", 2, "beyond"),
    ("down", 2, "beyond"),
    ("spread", -2, 1),
    ("down", 3, "own"),
    ("spread", -2, 2),
    ("up", 2, "opposite"),
    ("multiply", -2),
    ("spread", 2, 3),
    ("down", 2, "opposite"),
    ("spread", 2, 1),
    ("up", 3, "across"),
    ("down", 3, "across"),
    ("spread", 2, 2),
    ("multiply", 2),
    ("spread", -3, 3),
    ("up", 4, "own"),
    ("up", 3, "beyond"),
    ("spread", -3, 1),
    ("down", 3, "beyond"),
    ("spread", 3, 3),
    ("up", 3, "opposite"),
    ("spread", 3, 1),
    ("down", 3, "opposite"),
    ("spread", -3, 2),
    ("multiply", -3),
    ("up", 4, "across"),
    ("spread", -4, 3),
    ("up", 4, "beyond"),
    ("up", 4, "opposite"),
    ("spread", -4, 1),
    ("spread", 3, 2),
    ("multiply", 3),
    ("spread", -4, 2),
    ("mirror", -1),
    ("mirror", 1),
    ("multiply", -4),
)


def kernel(
    a_ref,
    out_ref,
    own,
    turned,
    rows_f32,
    rows_high,
    rows_low,
    cols,
    prod,
    own_sem,
    swap_s,
    swap_r,
    row_s,
    row_r,
    pass_s,
    pass_r,
    xa_s,
    xa_r,
    xf_s,
    xf_r,
    zl_s,
    zl_r,
    zs_s,
    zs_r,
    xb_s,
    xb_r,
    out_s,
    out_r,
    turned_out,
    turned_in,
    mirror_s,
    mirror_r,
):
    loop, xl = lax.axis_index("loop"), lax.axis_index("grp")
    c = loop % 2
    xh = (loop // 2) % 2
    z = (loop // 4) % NZ
    y = loop // 32
    x = xh * 2 + xl
    way = 1 - 2 * c

    def device(dx=0, dy=0, dz=0, dc=0):
        xx, yy, zz = (x + dx * way + NX) % NX, (y + dy * way + NY) % NY, (z + dz * way + NZ) % NZ
        return ((yy * NZ + zz) * 2 + xx // 2) * 2 + (c + dc) % NC, xx % 2

    sends = []

    def send(src, dst, s_sem, r_sem, to):
        copy = pltpu.make_async_remote_copy(
            src_ref=src, dst_ref=dst, send_sem=s_sem, recv_sem=r_sem, device_id=to, device_id_type=MESH
        )
        copy.start()
        sends.append(copy)

    mate = (loop, 1 - xl)

    def arrived(ref, r_sem, s_sem):
        pltpu.make_async_remote_copy(
            src_ref=ref, dst_ref=ref, send_sem=s_sem, recv_sem=r_sem, device_id=mate, device_id_type=MESH
        ).wait_recv()

    def piece(dx, zz, start=0, size=DEPTH):
        xx = (x + dx * way + NX) % NX
        return cols.at[zz, xx // 2, pl.ds(pl.multiple_of((xx % 2) * DEPTH + start, 8), size), :]

    def first(dx, zz):
        return piece(dx, zz, 0, FIRST)

    def rest(dx, zz):
        return piece(dx, zz, FIRST, DEPTH - FIRST)

    def origin(d):
        return (z + d * way + NZ) % NZ

    half = pl.ds(pl.multiple_of(xl * DEPTH, 128), DEPTH)
    other_half = pl.ds(pl.multiple_of((1 - xl) * DEPTH, 128), DEPTH)

    load = pltpu.make_async_copy(a_ref, own, own_sem)
    load.start()
    barrier = pltpu.get_barrier_semaphore()
    greeted = [device(dx=d) for d in (1, 2, 3)] + [device(dz=1), device(dz=-1), device(dc=1)]
    greeted += [device(dy=d, dc=e) for d in (1, 2, 3) for e in (0, 1)]
    greeted += [(device(dz=d)[0], 1 - xl) for d in (1, -1)]
    for who in greeted:
        pl.semaphore_signal(barrier, inc=1, device_id=who, device_id_type=MESH)
    load.wait()
    block = own[...]
    turned[...] = block.T
    rows_f32[SLOT[0, 0], :, half] = turned[pl.ds(pl.multiple_of(xl * OWN, 8), OWN), :]
    cols[z, xh, pl.ds(pl.multiple_of(xl * DEPTH, 8), DEPTH), :] = block
    pl.semaphore_wait(barrier, len(greeted))

    send(
        turned.at[pl.ds(pl.multiple_of((1 - xl) * OWN, 8), OWN), :],
        rows_f32.at[SLOT[0, 0], :, half],
        swap_s.at[0],
        swap_r.at[0],
        mate,
    )

    def give_rows(part, lanes):
        for to, there in ((1, 3), (-1, 1)):
            send(
                rows_f32.at[SLOT[0, 0], :, lanes],
                rows_f32.at[SLOT[there, 0], :, lanes],
                row_s.at[part, there - 1],
                row_r.at[part, there - 1],
                device(dy=to),
            )

    def rows_arrived(part, lanes, dy):
        slot = rows_f32.at[SLOT[dy, 0], :, lanes]
        arrived(slot, row_r.at[part, dy - 1], row_s.at[part, dy - 1])
        if dy == 3:
            send(slot, rows_f32.at[SLOT[2, 0], :, lanes], row_s.at[part, 1], row_r.at[part, 1], device(dy=1))

    def pass_rows(dy):
        send(
            rows_f32.at[SLOT[dy, 0]],
            rows_f32.at[SLOT[(4 - dy) % 4, 1]],
            pass_s.at[(4 - dy) % 4],
            pass_r.at[(4 - dy) % 4],
            device(dc=1),
        )

    def passed(dy):
        arrived(rows_f32.at[SLOT[dy, 1]], pass_r.at[dy], pass_s.at[dy])

    towards = (1 - 2 * xl) * way
    across, beyond = (towards + NX) % NX, (NX - towards) % NX
    up, down = device(dz=1), device(dz=-1)
    near_rows, far_rows = pl.ds(0, 4 * OWN), pl.ds(4 * OWN, 4 * OWN)
    mine = pl.ds(SLOT[0, 0] * TILES, TILES)

    def part_tiles(part):
        return pl.ds(part.start // 8, part.size // 8)

    def tiles_of(value):
        return value.reshape(value.shape[0] // 8, 8, WIDTH)


    def split(slots):
        part = pl.ds(slots.start * OWN, (slots.stop - slots.start) * OWN)
        rows = rows_f32[slots].reshape((slots.stop - slots.start) * OWN, 2 * DEPTH)
        high = rows.astype(jnp.bfloat16)
        rows_high[part, :] = high
        rows_low[part, :] = (rows - high.astype(jnp.float32)).astype(jnp.bfloat16)

    def product(part, block):
        block_high = block.astype(jnp.bfloat16)
        block_low = (block - block_high.astype(jnp.float32)).astype(jnp.bfloat16)
        value = jnp.dot(rows_high[part, :], block_high, preferred_element_type=jnp.float32)
        value += jnp.dot(rows_low[part, :], block_high, preferred_element_type=jnp.float32)
        value += jnp.dot(rows_high[part, :], block_low, preferred_element_type=jnp.float32)
        return value

    def deliver(group, src, dst, who):
        for dy, dc in who:
            there = (4 - dy) % 4 if dc == 0 else dy
            index = there * 2 + dc - 1
            k = SLOT[dy, dc]
            send(src(pl.ds(k * TILES, TILES)), dst, out_s.at[group, index], out_r.at[group, index], device(dy=dy, dc=dc))

    def own_plane(group, hh, part, who):
        prod[0, part_tiles(part), hh] = tiles_of(product(part, cols[z, hh]))
        deliver(group, lambda t: prod.at[0, t, hh], out_ref.at[:, y, z, hh, c], who)

    def plane_near(group, hh):
        if group == 0:
            split(slice(0, 4))
        own_plane(group, hh, near_rows, NEAR)

    def plane_far(group, hh):
        if group == 0:
            split(slice(4, 8))
        own_plane(group, hh, far_rows, FAR)
        if group == 0:
            row_ids = lax.broadcasted_iota(jnp.int32, (TILES, 8, WIDTH), 0) * 8 + xl * OWN
            row_ids += lax.broadcasted_iota(jnp.int32, (TILES, 8, WIDTH), 1)
            col_ids = lax.broadcasted_iota(jnp.int32, (TILES, 8, WIDTH), 2)
            factor = jnp.where(row_ids == col_ids, jnp.float32(1.0 + damping), jnp.float32(1.0))
            out_ref[:, y, z, hh, c] = prod[0, mine, hh] * factor
        else:
            out_ref[:, y, z, hh, c] = prod[0, mine, hh]

    def mirror_send(d):
        k, (there, _) = MIRRORED.index(d), device(dz=d)
        for far, xx in ((0, xl), (1, 1 - xl)):
            src = turned_out.at[k, pl.ds(pl.multiple_of(xx * OWN, 8), OWN), :]
            send(src, turned_in.at[k, xl], mirror_s.at[k, far], mirror_r.at[k, far], (there, xx))

    def mirror_arrived(d):
        k, zz = MIRRORED.index(d), origin(-d)
        for far, xx in ((0, xl), (1, 1 - xl)):
            arrived(turned_in.at[k, xx], mirror_r.at[k, far], mirror_s.at[k, far])
        for (dy, dc), slot in SLOT.items():
            if dy:
                part = slice(slot * OWN, (slot + 1) * OWN)
                strip = jnp.concatenate([turned_in[k, 0][:, part], turned_in[k, 1][:, part]], axis=1)
                out_ref[:, (y + dy * way + NY) % NY, zz, xh, (c + dc) % NC] = tiles_of(strip)

    def multiply(d):
        unit, zz = UNITS.index(d) + 1, origin(d)
        value = product(pl.ds(0, 8 * OWN), jnp.concatenate([cols[zz, 0], cols[zz, 1]], axis=1))
        prod[unit, :, 0] = tiles_of(value[:, :WIDTH])
        prod[unit, :, 1] = tiles_of(value[:, WIDTH:])
        if d in MIRRORED:
            deliver(unit, lambda t: prod.at[unit, t, 1 - xh], out_ref.at[:, y, zz, 1 - xh, c], NEAR + FAR[:2])
            deliver(unit, lambda t: prod.at[unit, t], out_ref.at[:, y, zz, :, c], FAR[2:])
            turned_out[MIRRORED.index(d)] = prod[unit, : 6 * TILES, xh].reshape(6 * OWN, WIDTH).T
            mirror_send(d)
        else:
            deliver(unit, lambda t: prod.at[unit, t], out_ref.at[:, y, zz, :, c], NEAR + FAR)
        out_ref[:, y, zz, 0, c] = prod[unit, mine, 0]
        out_ref[:, y, zz, 1, c] = prod[unit, mine, 1]

    def ring_start(dx, part):
        send(part, part, zl_s.at[0, dx], zl_r.at[0, dx], up)
        send(part, part, zs_s.at[0, dx], zs_r.at[0, dx], down)

    def ring_up(d, dx):
        part = piece(0, origin(-d)) if isinstance(dx, int) and dx == 0 else first(dx, origin(-d))
        arrived(part, zl_r.at[d - 1, dx], zl_s.at[d - 1, dx])
        if d < 4:
            send(part, part, zl_s.at[d, dx], zl_r.at[d, dx], up)

    def ring_down(d, dx):
        part = piece(0, origin(d)) if isinstance(dx, int) and dx == 0 else first(dx, origin(d))
        arrived(part, zs_r.at[d - 1, dx], zs_s.at[d - 1, dx])
        if d < 3:
            send(part, part, zs_s.at[d, dx], zs_r.at[d, dx], down)

    def spread(d):
        part, unit = rest(0, origin(d)), UNITS.index(d)
        for to, there in ((1, 3), (-1, 1)):
            send(part, part, xb_s.at[unit, there - 1], xb_r.at[unit, there - 1], device(dx=to))
        if d in DIRECT:
            send(part, part, xb_s.at[unit, 1], xb_r.at[unit, 1], device(dx=2))

    def spread_came(d, dx):
        part, unit = rest(dx, origin(d)), UNITS.index(d)
        arrived(part, xb_r.at[unit, dx - 1], xb_s.at[unit, dx - 1])
        if dx == 3 and d not in DIRECT:
            send(part, part, xb_s.at[unit, 1], xb_r.at[unit, 1], device(dx=1))

    give_rows(0, half)
    for part, s_sem, r_sem in ((first(0, z), xa_s, xa_r), (rest(0, z), xf_s, xf_r)):
        send(part, part, s_sem.at[1 + towards], r_sem.at[1 + towards], device(dx=towards))
        if s_sem is xa_s:
            ring_start(0, piece(0, z))
        send(part, part, s_sem.at[1 - towards], r_sem.at[1 - towards], device(dx=-towards))
        send(part, part, s_sem.at[1], r_sem.at[1], device(dx=2))

    for event in ORDER:
        kind, at = event[0], event[1:]
        if kind == "swap":
            arrived(rows_f32.at[SLOT[0, 0], :, other_half], swap_r.at[0], swap_s.at[0])
            give_rows(1, other_half)
            pass_rows(0)
        elif kind == "rows":
            rows_arrived(at[0], (half, other_half)[at[0]], at[1])
            if at[0] == 1:
                pass_rows(at[1])
        elif kind == "passed":
            passed(at[0])
        elif kind in ("first", "rest"):
            dx = {"across": across, "beyond": beyond, "opposite": 2}[at[0]]
            if kind == "first":
                arrived(first(dx, z), xa_r.at[dx - 1], xa_s.at[dx - 1])
                ring_start(dx, first(dx, z))
            else:
                arrived(rest(dx, z), xf_r.at[dx - 1], xf_s.at[dx - 1])
        elif kind in ("up", "down"):
            dx = {"own": 0, "across": across, "beyond": beyond, "opposite": 2}[at[1]]
            (ring_up if kind == "up" else ring_down)(at[0], dx)
            if at[1] == "own":
                spread(-at[0] if kind == "up" else at[0])
        elif kind == "spread":
            spread_came(at[0], at[1])
        elif kind == "mirror":
            mirror_arrived(at[0])
        elif kind == "near":
            plane_near(at[0], xh if at[0] == 0 else 1 - xh)
        elif kind == "far":
            plane_far(at[0], xh if at[0] == 0 else 1 - xh)
        else:
            multiply(at[0])

    for dy, dc in NEAR + FAR:
        index = dy * 2 + dc - 1
        yy, cc = (y + dy * way + NY) % NY, (c + dc) % NC
        for group, hh in ((0, xh), (8, 1 - xh)):
            arrived(out_ref.at[:, yy, z, hh, cc], out_r.at[group, index], out_s.at[group, index])
        for unit, d in enumerate(UNITS):
            zz = (z + d * (1 - 2 * cc) + NZ) % NZ
            part = out_ref.at[:, yy, zz, 1 - xh, cc] if dy and d in MIRRORED else out_ref.at[:, yy, zz, :, cc]
            arrived(part, out_r.at[unit + 1, index], out_s.at[unit + 1, index])
    for copy in sends:
        copy.wait_send()


def per_device(jacobian):
    dma = pltpu.SemaphoreType.DMA
    tiles = pl.pallas_call(
        kernel,
        name="gather_multiply_scatter",
        out_shape=jax.ShapeDtypeStruct((TILES, NY, NZ, 2, NC, 8, WIDTH), jnp.float32),
        in_specs=[pl.BlockSpec(memory_space=pltpu.HBM)],
        out_specs=pl.BlockSpec(memory_space=pltpu.VMEM),
        scratch_shapes=[
            pltpu.VMEM((DEPTH, WIDTH), jnp.float32),
            pltpu.VMEM((WIDTH, DEPTH), jnp.float32),
            pltpu.VMEM((NY * NC, OWN, 2 * DEPTH), jnp.float32),
            pltpu.VMEM((NY * NC * OWN, 2 * DEPTH), jnp.bfloat16),
            pltpu.VMEM((NY * NC * OWN, 2 * DEPTH), jnp.bfloat16),
            pltpu.VMEM((NZ, 2, 2 * DEPTH, WIDTH), jnp.float32),
            pltpu.VMEM((NZ, NY * NC * TILES, 2, 8, WIDTH), jnp.float32),
            dma,
            dma((1,)),
            dma((1,)),
            dma((2, 3)),
            dma((2, 3)),
            dma((4,)),
            dma((4,)),
            dma((3,)),
            dma((3,)),
            dma((3,)),
            dma((3,)),
            dma((4, 4)),
            dma((4, 4)),
            dma((3, 4)),
            dma((3, 4)),
            dma((7, 3)),
            dma((7, 3)),
            dma((9, 7)),
            dma((9, 7)),
            pltpu.VMEM((len(MIRRORED), WIDTH, 6 * OWN), jnp.float32),
            pltpu.VMEM((len(MIRRORED), 2, OWN, 6 * OWN), jnp.float32),
            dma((len(MIRRORED), 2)),
            dma((len(MIRRORED), 2)),
        ],
        compiler_params=pltpu.CompilerParams(
            collective_id=0, has_side_effects=True, vmem_limit_bytes=48 * 2**20
        ),
    )(pltpu.with_memory_space_constraint(jacobian, pltpu.HBM))
    tiles = tiles.reshape(TILES, NY * NZ * 2 * NC, 8, WIDTH)
    return jnp.transpose(tiles, (0, 2, 1, 3)).reshape(OWN, NY * NZ * 2 * NC * WIDTH)


def solution(mesh):
    return jax.shard_map(
        per_device,
        mesh=mesh,
        in_specs=(P("grp", "loop"),),
        out_specs=P(("loop", "grp"), None),
        check_vma=False,
    )
```

```python
import jax
import jax.numpy as jnp
from jax import lax
from jax.experimental import pallas as pl
from jax.experimental.pallas import tpu as pltpu
from jax.sharding import PartitionSpec as P

damping = 0.1
MESH = pl.DeviceIdType.MESH
NX, NY, NZ, NC = 4, 4, 8, 2
DEPTH, WIDTH, OWN = 384, 128, 64
TILES = OWN // 8
FIRST = 176


SLOT = {(1, 0): 0, (3, 0): 1, (1, 1): 2, (3, 1): 3, (2, 0): 4, (2, 1): 5, (0, 0): 6, (0, 1): 7}
NEAR, FAR = ((1, 0), (3, 0), (1, 1), (3, 1)), ((2, 0), (2, 1), (0, 1))
UNITS = (-1, 1, -2, 2, -3, 3, -4)
MIRRORED = (-1, 1)
DIRECT = (-1, 1, -2, 2, -3, 3)
ORDER = (
    ("swap",),
    ("rows", 0, 3),
    ("first", "across"),
    ("rows", 0, 1),
    ("up", 1, "own"),
    ("passed", 0),
    ("first", "beyond"),
    ("rows", 1, 3),
    ("rows", 1, 1),
    ("down", 1, "own"),
    ("passed", 1),
    ("first", "opposite"),
    ("rows", 0, 2),
    ("up", 1, "across"),
    ("rest", "across"),
    ("passed", 3),
    ("near", 0),
    ("rows", 1, 2),
    ("down", 1, "across"),
    ("rest", "beyond"),
    ("passed", 2),
    ("far", 0),
    ("up", 2, "own"),
    ("up", 1, "beyond"),
    ("rest", "opposite"),
    ("near", 8),
    ("spread", -1, 3),
    ("far", 8),
    ("down", 1, "beyond"),
    ("spread", -1, 1),
    ("down", 2, "own"),
    ("up", 1, "opposite"),
    ("spread", -1, 2),
    ("multiply", -1),
    ("down", 1, "opposite"),
    ("spread", 1, 3),
    ("up", 2, "across"),
    ("spread", 1, 1),
    ("down", 2, "across"),
    ("up", 3, "own"),
    ("spread", 1, 2),
    ("multiply", 1),
    ("spread", -2, 3),
    ("up", 2, "beyond"),
    ("down", 2, "beyond"),
    ("spread", -2, 1),
    ("down", 3, "own"),
    ("spread", -2, 2),
    ("up", 2, "opposite"),
    ("multiply", -2),
    ("spread", 2, 3),
    ("down", 2, "opposite"),
    ("spread", 2, 1),
    ("up", 3, "across"),
    ("down", 3, "across"),
    ("spread", 2, 2),
    ("multiply", 2),
    ("spread", -3, 3),
    ("up", 4, "own"),
    ("up", 3, "beyond"),
    ("spread", -3, 1),
    ("down", 3, "beyond"),
    ("up", 3, "opposite"),
    ("down", 3, "opposite"),
    ("spread", -3, 2),
    ("multiply", -3),
    ("spread", 3, 3),
    ("up", 4, "across"),
    ("spread", 3, 1),
    ("up", 4, "beyond"),
    ("up", 4, "opposite"),
    ("spread", 3, 2),
    ("multiply", 3),
    ("mirror_send", -1),
    ("mirror_send", 1),
    ("spread", -4, 3),
    ("spread", -4, 1),
    ("spread", -4, 2),
    ("multiply", -4),
    ("mirror", -1),
    ("mirror", 1),
)


def kernel(
    a_ref,
    out_ref,
    own,
    turned,
    rows_f32,
    rows_high,
    rows_low,
    cols,
    prod,
    own_sem,
    swap_s,
    swap_r,
    row_s,
    row_r,
    pass_s,
    pass_r,
    xa_s,
    xa_r,
    xf_s,
    xf_r,
    zl_s,
    zl_r,
    zs_s,
    zs_r,
    xb_s,
    xb_r,
    out_s,
    out_r,
    turned_out,
    turned_in,
    mirror_s,
    mirror_r,
):
    loop, xl = lax.axis_index("loop"), lax.axis_index("grp")
    c = loop % 2
    xh = (loop // 2) % 2
    z = (loop // 4) % NZ
    y = loop // 32
    x = xh * 2 + xl
    way = 1 - 2 * c

    def device(dx=0, dy=0, dz=0, dc=0):
        xx, yy, zz = (x + dx * way + NX) % NX, (y + dy * way + NY) % NY, (z + dz * way + NZ) % NZ
        return ((yy * NZ + zz) * 2 + xx // 2) * 2 + (c + dc) % NC, xx % 2

    sends = []

    def send(src, dst, s_sem, r_sem, to):
        copy = pltpu.make_async_remote_copy(
            src_ref=src, dst_ref=dst, send_sem=s_sem, recv_sem=r_sem, device_id=to, device_id_type=MESH
        )
        copy.start()
        sends.append(copy)

    mate = (loop, 1 - xl)

    def arrived(ref, r_sem, s_sem):
        pltpu.make_async_remote_copy(
            src_ref=ref, dst_ref=ref, send_sem=s_sem, recv_sem=r_sem, device_id=mate, device_id_type=MESH
        ).wait_recv()

    def piece(dx, zz, start=0, size=DEPTH):
        xx = (x + dx * way + NX) % NX
        return cols.at[zz, xx // 2, pl.ds(pl.multiple_of((xx % 2) * DEPTH + start, 8), size), :]

    def first(dx, zz):
        return piece(dx, zz, 0, FIRST)

    def rest(dx, zz):
        return piece(dx, zz, FIRST, DEPTH - FIRST)

    def origin(d):
        return (z + d * way + NZ) % NZ

    half = pl.ds(pl.multiple_of(xl * DEPTH, 128), DEPTH)
    other_half = pl.ds(pl.multiple_of((1 - xl) * DEPTH, 128), DEPTH)

    load = pltpu.make_async_copy(a_ref, own, own_sem)
    load.start()
    barrier = pltpu.get_barrier_semaphore()
    greeted = [device(dx=d) for d in (1, 2, 3)] + [device(dz=1), device(dz=-1), device(dc=1)]
    greeted += [device(dy=d, dc=e) for d in (1, 2, 3) for e in (0, 1)]
    greeted += [(device(dz=d)[0], 1 - xl) for d in (1, -1)]
    for who in greeted:
        pl.semaphore_signal(barrier, inc=1, device_id=who, device_id_type=MESH)
    load.wait()
    block = own[...]
    turned[...] = block.T
    rows_f32[SLOT[0, 0], :, half] = turned[pl.ds(pl.multiple_of(xl * OWN, 8), OWN), :]
    cols[z, xh, pl.ds(pl.multiple_of(xl * DEPTH, 8), DEPTH), :] = block
    pl.semaphore_wait(barrier, len(greeted))

    send(
        turned.at[pl.ds(pl.multiple_of((1 - xl) * OWN, 8), OWN), :],
        rows_f32.at[SLOT[0, 0], :, half],
        swap_s.at[0],
        swap_r.at[0],
        mate,
    )

    def give_rows(part, lanes):
        for to, there in ((1, 3), (-1, 1)):
            send(
                rows_f32.at[SLOT[0, 0], :, lanes],
                rows_f32.at[SLOT[there, 0], :, lanes],
                row_s.at[part, there - 1],
                row_r.at[part, there - 1],
                device(dy=to),
            )

    def rows_arrived(part, lanes, dy):
        slot = rows_f32.at[SLOT[dy, 0], :, lanes]
        arrived(slot, row_r.at[part, dy - 1], row_s.at[part, dy - 1])
        if dy == 3:
            send(slot, rows_f32.at[SLOT[2, 0], :, lanes], row_s.at[part, 1], row_r.at[part, 1], device(dy=1))

    def pass_rows(dy):
        send(
            rows_f32.at[SLOT[dy, 0]],
            rows_f32.at[SLOT[(4 - dy) % 4, 1]],
            pass_s.at[(4 - dy) % 4],
            pass_r.at[(4 - dy) % 4],
            device(dc=1),
        )

    def passed(dy):
        arrived(rows_f32.at[SLOT[dy, 1]], pass_r.at[dy], pass_s.at[dy])

    towards = (1 - 2 * xl) * way
    across, beyond = (towards + NX) % NX, (NX - towards) % NX
    up, down = device(dz=1), device(dz=-1)
    near_rows, far_rows = pl.ds(0, 4 * OWN), pl.ds(4 * OWN, 4 * OWN)
    mine = pl.ds(SLOT[0, 0] * TILES, TILES)

    def part_tiles(part):
        return pl.ds(part.start // 8, part.size // 8)

    def tiles_of(value):
        return value.reshape(value.shape[0] // 8, 8, WIDTH)


    def split(slots):
        part = pl.ds(slots.start * OWN, (slots.stop - slots.start) * OWN)
        rows = rows_f32[slots].reshape((slots.stop - slots.start) * OWN, 2 * DEPTH)
        high = rows.astype(jnp.bfloat16)
        rows_high[part, :] = high
        rows_low[part, :] = (rows - high.astype(jnp.float32)).astype(jnp.bfloat16)

    def product(part, block):
        block_high = block.astype(jnp.bfloat16)
        block_low = (block - block_high.astype(jnp.float32)).astype(jnp.bfloat16)
        value = jnp.dot(rows_high[part, :], block_high, preferred_element_type=jnp.float32)
        value += jnp.dot(rows_low[part, :], block_high, preferred_element_type=jnp.float32)
        value += jnp.dot(rows_high[part, :], block_low, preferred_element_type=jnp.float32)
        return value

    def deliver(group, src, dst, who):
        for dy, dc in who:
            there = (4 - dy) % 4 if dc == 0 else dy
            index = there * 2 + dc - 1
            k = SLOT[dy, dc]
            send(src(pl.ds(k * TILES, TILES)), dst, out_s.at[group, index], out_r.at[group, index], device(dy=dy, dc=dc))

    def own_plane(group, hh, part, who):
        prod[0, part_tiles(part), hh] = tiles_of(product(part, cols[z, hh]))
        deliver(group, lambda t: prod.at[0, t, hh], out_ref.at[:, y, z, hh, c], who)

    def plane_near(group, hh):
        if group == 0:
            split(slice(0, 4))
        own_plane(group, hh, near_rows, NEAR)

    def plane_far(group, hh):
        if group == 0:
            split(slice(4, 8))
        own_plane(group, hh, far_rows, FAR)
        if group == 0:
            row_ids = lax.broadcasted_iota(jnp.int32, (TILES, 8, WIDTH), 0) * 8 + xl * OWN
            row_ids += lax.broadcasted_iota(jnp.int32, (TILES, 8, WIDTH), 1)
            col_ids = lax.broadcasted_iota(jnp.int32, (TILES, 8, WIDTH), 2)
            factor = jnp.where(row_ids == col_ids, jnp.float32(1.0 + damping), jnp.float32(1.0))
            out_ref[:, y, z, hh, c] = prod[0, mine, hh] * factor
        else:
            out_ref[:, y, z, hh, c] = prod[0, mine, hh]

    def mirror_send(d):
        k, (there, _) = MIRRORED.index(d), device(dz=d)
        turned_out[k] = prod[UNITS.index(d) + 1, : 6 * TILES, xh].reshape(6 * OWN, WIDTH).T
        for far, xx in ((0, xl), (1, 1 - xl)):
            src = turned_out.at[k, pl.ds(pl.multiple_of(xx * OWN, 8), OWN), :]
            send(src, turned_in.at[k, xl], mirror_s.at[k, far], mirror_r.at[k, far], (there, xx))

    def mirror_arrived(d):
        k, zz = MIRRORED.index(d), origin(-d)
        for far, xx in ((0, xl), (1, 1 - xl)):
            arrived(turned_in.at[k, xx], mirror_r.at[k, far], mirror_s.at[k, far])
        for (dy, dc), slot in SLOT.items():
            if dy:
                part = slice(slot * OWN, (slot + 1) * OWN)
                strip = jnp.concatenate([turned_in[k, 0][:, part], turned_in[k, 1][:, part]], axis=1)
                out_ref[:, (y + dy * way + NY) % NY, zz, xh, (c + dc) % NC] = tiles_of(strip)

    def multiply(d):
        unit, zz = UNITS.index(d) + 1, origin(d)
        value = product(pl.ds(0, 8 * OWN), jnp.concatenate([cols[zz, 0], cols[zz, 1]], axis=1))
        prod[unit, :, 0] = tiles_of(value[:, :WIDTH])
        prod[unit, :, 1] = tiles_of(value[:, WIDTH:])
        if d in MIRRORED:
            deliver(unit, lambda t: prod.at[unit, t, 1 - xh], out_ref.at[:, y, zz, 1 - xh, c], NEAR + FAR[:2])
            deliver(unit, lambda t: prod.at[unit, t], out_ref.at[:, y, zz, :, c], FAR[2:])
        else:
            deliver(unit, lambda t: prod.at[unit, t], out_ref.at[:, y, zz, :, c], NEAR + FAR)
        out_ref[:, y, zz, 0, c] = prod[unit, mine, 0]
        out_ref[:, y, zz, 1, c] = prod[unit, mine, 1]

    def ring_start(dx, part):
        send(part, part, zl_s.at[0, dx], zl_r.at[0, dx], up)
        send(part, part, zs_s.at[0, dx], zs_r.at[0, dx], down)

    def ring_up(d, dx):
        part = piece(0, origin(-d)) if isinstance(dx, int) and dx == 0 else first(dx, origin(-d))
        arrived(part, zl_r.at[d - 1, dx], zl_s.at[d - 1, dx])
        if d < 4:
            send(part, part, zl_s.at[d, dx], zl_r.at[d, dx], up)

    def ring_down(d, dx):
        part = piece(0, origin(d)) if isinstance(dx, int) and dx == 0 else first(dx, origin(d))
        arrived(part, zs_r.at[d - 1, dx], zs_s.at[d - 1, dx])
        if d < 3:
            send(part, part, zs_s.at[d, dx], zs_r.at[d, dx], down)

    def spread(d):
        part, unit = rest(0, origin(d)), UNITS.index(d)
        for to, there in ((1, 3), (-1, 1)):
            send(part, part, xb_s.at[unit, there - 1], xb_r.at[unit, there - 1], device(dx=to))
        if d in DIRECT:
            send(part, part, xb_s.at[unit, 1], xb_r.at[unit, 1], device(dx=2))

    def spread_came(d, dx):
        part, unit = rest(dx, origin(d)), UNITS.index(d)
        arrived(part, xb_r.at[unit, dx - 1], xb_s.at[unit, dx - 1])
        if dx == 3 and d not in DIRECT:
            send(part, part, xb_s.at[unit, 1], xb_r.at[unit, 1], device(dx=1))

    give_rows(0, half)
    for part, s_sem, r_sem in ((first(0, z), xa_s, xa_r), (rest(0, z), xf_s, xf_r)):
        send(part, part, s_sem.at[1 + towards], r_sem.at[1 + towards], device(dx=towards))
        if s_sem is xa_s:
            ring_start(0, piece(0, z))
        send(part, part, s_sem.at[1 - towards], r_sem.at[1 - towards], device(dx=-towards))
        send(part, part, s_sem.at[1], r_sem.at[1], device(dx=2))

    for event in ORDER:
        kind, at = event[0], event[1:]
        if kind == "swap":
            arrived(rows_f32.at[SLOT[0, 0], :, other_half], swap_r.at[0], swap_s.at[0])
            give_rows(1, other_half)
            pass_rows(0)
        elif kind == "rows":
            rows_arrived(at[0], (half, other_half)[at[0]], at[1])
            if at[0] == 1:
                pass_rows(at[1])
        elif kind == "passed":
            passed(at[0])
        elif kind in ("first", "rest"):
            dx = {"across": across, "beyond": beyond, "opposite": 2}[at[0]]
            if kind == "first":
                arrived(first(dx, z), xa_r.at[dx - 1], xa_s.at[dx - 1])
                ring_start(dx, first(dx, z))
            else:
                arrived(rest(dx, z), xf_r.at[dx - 1], xf_s.at[dx - 1])
        elif kind in ("up", "down"):
            dx = {"own": 0, "across": across, "beyond": beyond, "opposite": 2}[at[1]]
            (ring_up if kind == "up" else ring_down)(at[0], dx)
            if at[1] == "own":
                spread(-at[0] if kind == "up" else at[0])
        elif kind == "spread":
            spread_came(at[0], at[1])
        elif kind == "mirror_send":
            mirror_send(at[0])
        elif kind == "mirror":
            mirror_arrived(at[0])
        elif kind == "near":
            plane_near(at[0], xh if at[0] == 0 else 1 - xh)
        elif kind == "far":
            plane_far(at[0], xh if at[0] == 0 else 1 - xh)
        else:
            multiply(at[0])

    last = len(NEAR + FAR)
    for copy in sends[:-last]:
        copy.wait_send()
    for group, d in ((0, 0), (8, 0), *((unit + 1, d) for unit, d in enumerate(UNITS))):
        for dy, dc in NEAR + FAR:
            index = dy * 2 + dc - 1
            yy, cc = (y + dy * way + NY) % NY, (c + dc) % NC
            zz = (z + d * (1 - 2 * cc) + NZ) % NZ
            if d == 0:
                part = out_ref.at[:, yy, z, xh if group == 0 else 1 - xh, cc]
            elif dy and d in MIRRORED:
                part = out_ref.at[:, yy, zz, 1 - xh, cc]
            else:
                part = out_ref.at[:, yy, zz, :, cc]
            arrived(part, out_r.at[group, index], out_s.at[group, index])
    for copy in sends[-last:]:
        copy.wait_send()


def per_device(jacobian):
    dma = pltpu.SemaphoreType.DMA
    tiles = pl.pallas_call(
        kernel,
        name="gather_multiply_scatter",
        out_shape=jax.ShapeDtypeStruct((TILES, NY, NZ, 2, NC, 8, WIDTH), jnp.float32),
        in_specs=[pl.BlockSpec(memory_space=pltpu.HBM)],
        out_specs=pl.BlockSpec(memory_space=pltpu.VMEM),
        scratch_shapes=[
            pltpu.VMEM((DEPTH, WIDTH), jnp.float32),
            pltpu.VMEM((WIDTH, DEPTH), jnp.float32),
            pltpu.VMEM((NY * NC, OWN, 2 * DEPTH), jnp.float32),
            pltpu.VMEM((NY * NC * OWN, 2 * DEPTH), jnp.bfloat16),
            pltpu.VMEM((NY * NC * OWN, 2 * DEPTH), jnp.bfloat16),
            pltpu.VMEM((NZ, 2, 2 * DEPTH, WIDTH), jnp.float32),
            pltpu.VMEM((NZ, NY * NC * TILES, 2, 8, WIDTH), jnp.float32),
            dma,
            dma((1,)),
            dma((1,)),
            dma((2, 3)),
            dma((2, 3)),
            dma((4,)),
            dma((4,)),
            dma((3,)),
            dma((3,)),
            dma((3,)),
            dma((3,)),
            dma((4, 4)),
            dma((4, 4)),
            dma((3, 4)),
            dma((3, 4)),
            dma((7, 3)),
            dma((7, 3)),
            dma((9, 7)),
            dma((9, 7)),
            pltpu.VMEM((len(MIRRORED), WIDTH, 6 * OWN), jnp.float32),
            pltpu.VMEM((len(MIRRORED), 2, OWN, 6 * OWN), jnp.float32),
            dma((len(MIRRORED), 2)),
            dma((len(MIRRORED), 2)),
        ],
        compiler_params=pltpu.CompilerParams(
            collective_id=0, has_side_effects=True, vmem_limit_bytes=48 * 2**20
        ),
    )(pltpu.with_memory_space_constraint(jacobian, pltpu.HBM))
    tiles = tiles.reshape(TILES, NY * NZ * 2 * NC, 8, WIDTH)
    return jnp.transpose(tiles, (0, 2, 1, 3)).reshape(OWN, NY * NZ * 2 * NC * WIDTH)


def solution(mesh):
    return jax.shard_map(
        per_device,
        mesh=mesh,
        in_specs=(P("grp", "loop"),),
        out_specs=P(("loop", "grp"), None),
        check_vma=False,
    )
```

```python
import jax
import jax.numpy as jnp
from jax import lax
from jax.experimental import pallas as pl
from jax.experimental.pallas import tpu as pltpu
from jax.sharding import PartitionSpec as P

damping = 0.1
MESH = pl.DeviceIdType.MESH
NX, NY, NZ, NC = 4, 4, 8, 2
DEPTH, WIDTH, OWN = 384, 128, 64
TILES = OWN // 8
FIRST = 176


SLOT = {(1, 0): 0, (3, 0): 1, (1, 1): 2, (3, 1): 3, (2, 0): 4, (2, 1): 5, (0, 0): 6, (0, 1): 7}
NEAR, FAR = ((1, 0), (3, 0), (1, 1), (3, 1)), ((2, 0), (2, 1), (0, 1))
UNITS = (-1, 1, -2, 2, -3, 3, -4)
MIRRORED = (-1, 1)
DIRECT = (-1, 1, -2, 2, -3, 3)
ORDER = (
    ("swap",),
    ("rows", 0, 3),
    ("first", "across"),
    ("rows", 0, 1),
    ("up", 1, "own"),
    ("passed", 0),
    ("first", "beyond"),
    ("rows", 1, 3),
    ("rows", 1, 1),
    ("down", 1, "own"),
    ("passed", 1),
    ("first", "opposite"),
    ("rows", 0, 2),
    ("up", 1, "across"),
    ("rest", "across"),
    ("passed", 3),
    ("near", 0),
    ("rows", 1, 2),
    ("down", 1, "across"),
    ("rest", "beyond"),
    ("passed", 2),
    ("far", 0),
    ("up", 2, "own"),
    ("up", 1, "beyond"),
    ("rest", "opposite"),
    ("near", 8),
    ("spread", -1, 3),
    ("far", 8),
    ("down", 1, "beyond"),
    ("spread", -1, 1),
    ("down", 2, "own"),
    ("up", 1, "opposite"),
    ("spread", -1, 2),
    ("multiply", -1),
    ("down", 1, "opposite"),
    ("spread", 1, 3),
    ("up", 2, "across"),
    ("spread", 1, 1),
    ("down", 2, "across"),
    ("up", 3, "own"),
    ("spread", 1, 2),
    ("multiply", 1),
    ("spread", -2, 3),
    ("up", 2, "beyond"),
    ("down", 2, "beyond"),
    ("spread", -2, 1),
    ("down", 3, "own"),
    ("spread", -2, 2),
    ("up", 2, "opposite"),
    ("multiply", -2),
    ("spread", 2, 3),
    ("down", 2, "opposite"),
    ("spread", 2, 1),
    ("up", 3, "across"),
    ("down", 3, "across"),
    ("spread", 2, 2),
    ("multiply", 2),
    ("spread", -3, 3),
    ("up", 4, "own"),
    ("up", 3, "beyond"),
    ("spread", -3, 1),
    ("down", 3, "beyond"),
    ("up", 3, "opposite"),
    ("down", 3, "opposite"),
    ("spread", -3, 2),
    ("multiply", -3),
    ("spread", 3, 3),
    ("up", 4, "across"),
    ("spread", 3, 1),
    ("up", 4, "beyond"),
    ("up", 4, "opposite"),
    ("spread", 3, 2),
    ("multiply", 3),
    ("mirror_send", -1),
    ("mirror_send", 1),
    ("spread", -4, 3),
    ("spread", -4, 1),
    ("spread", -4, 2),
    ("multiply", -4),
    ("mirror", -1),
    ("mirror", 1),
)


def kernel(
    a_ref,
    out_ref,
    own,
    turned,
    rows_f32,
    rows_high,
    rows_low,
    cols,
    prod,
    own_sem,
    swap_s,
    swap_r,
    row_s,
    row_r,
    pass_s,
    pass_r,
    xa_s,
    xa_r,
    xf_s,
    xf_r,
    zl_s,
    zl_r,
    zs_s,
    zs_r,
    xb_s,
    xb_r,
    out_s,
    out_r,
    turned_out,
    turned_in,
    mirror_s,
    mirror_r,
):
    loop, xl = lax.axis_index("loop"), lax.axis_index("grp")
    c = loop % 2
    xh = (loop // 2) % 2
    z = (loop // 4) % NZ
    y = loop // 32
    x = xh * 2 + xl
    way = 1 - 2 * c

    def device(dx=0, dy=0, dz=0, dc=0):
        xx, yy, zz = (x + dx * way + NX) % NX, (y + dy * way + NY) % NY, (z + dz * way + NZ) % NZ
        return ((yy * NZ + zz) * 2 + xx // 2) * 2 + (c + dc) % NC, xx % 2

    sends = []

    def send(src, dst, s_sem, r_sem, to):
        copy = pltpu.make_async_remote_copy(
            src_ref=src, dst_ref=dst, send_sem=s_sem, recv_sem=r_sem, device_id=to, device_id_type=MESH
        )
        copy.start()
        sends.append(copy)

    mate = (loop, 1 - xl)

    def arrived(ref, r_sem, s_sem):
        pltpu.make_async_remote_copy(
            src_ref=ref, dst_ref=ref, send_sem=s_sem, recv_sem=r_sem, device_id=mate, device_id_type=MESH
        ).wait_recv()

    def piece(dx, zz, start=0, size=DEPTH):
        xx = (x + dx * way + NX) % NX
        return cols.at[zz, xx // 2, pl.ds(pl.multiple_of((xx % 2) * DEPTH + start, 8), size), :]

    def first(dx, zz):
        return piece(dx, zz, 0, FIRST)

    def rest(dx, zz):
        return piece(dx, zz, FIRST, DEPTH - FIRST)

    def origin(d):
        return (z + d * way + NZ) % NZ

    half = pl.ds(pl.multiple_of(xl * DEPTH, 128), DEPTH)
    other_half = pl.ds(pl.multiple_of((1 - xl) * DEPTH, 128), DEPTH)

    load = pltpu.make_async_copy(a_ref, own, own_sem)
    load.start()
    barrier = pltpu.get_barrier_semaphore()
    greeted = [device(dx=d) for d in (1, 2, 3)] + [device(dz=1), device(dz=-1), device(dc=1)]
    greeted += [device(dy=d, dc=e) for d in (1, 2, 3) for e in (0, 1)]
    greeted += [(device(dz=d)[0], 1 - xl) for d in (1, -1)]
    for who in greeted:
        pl.semaphore_signal(barrier, inc=1, device_id=who, device_id_type=MESH)
    load.wait()
    block = own[...]
    turned[...] = block.T
    rows_f32[SLOT[0, 0], :, half] = turned[pl.ds(pl.multiple_of(xl * OWN, 8), OWN), :]
    cols[z, xh, pl.ds(pl.multiple_of(xl * DEPTH, 8), DEPTH), :] = block
    pl.semaphore_wait(barrier, len(greeted))

    send(
        turned.at[pl.ds(pl.multiple_of((1 - xl) * OWN, 8), OWN), :],
        rows_f32.at[SLOT[0, 0], :, half],
        swap_s.at[0],
        swap_r.at[0],
        mate,
    )

    def give_rows(part, lanes):
        for to, there in ((1, 3), (-1, 1), (2, 2)):
            send(
                rows_f32.at[SLOT[0, 0], :, lanes],
                rows_f32.at[SLOT[there, 0], :, lanes],
                row_s.at[part, there - 1],
                row_r.at[part, there - 1],
                device(dy=to),
            )

    def rows_arrived(part, lanes, dy):
        slot = rows_f32.at[SLOT[dy, 0], :, lanes]
        arrived(slot, row_r.at[part, dy - 1], row_s.at[part, dy - 1])

    def pass_rows(dy):
        send(
            rows_f32.at[SLOT[dy, 0]],
            rows_f32.at[SLOT[(4 - dy) % 4, 1]],
            pass_s.at[(4 - dy) % 4],
            pass_r.at[(4 - dy) % 4],
            device(dc=1),
        )

    def passed(dy):
        arrived(rows_f32.at[SLOT[dy, 1]], pass_r.at[dy], pass_s.at[dy])

    towards = (1 - 2 * xl) * way
    across, beyond = (towards + NX) % NX, (NX - towards) % NX
    up, down = device(dz=1), device(dz=-1)
    near_rows, far_rows = pl.ds(0, 4 * OWN), pl.ds(4 * OWN, 4 * OWN)
    mine = pl.ds(SLOT[0, 0] * TILES, TILES)

    def part_tiles(part):
        return pl.ds(part.start // 8, part.size // 8)

    def tiles_of(value):
        return value.reshape(value.shape[0] // 8, 8, WIDTH)


    def split(slots):
        part = pl.ds(slots.start * OWN, (slots.stop - slots.start) * OWN)
        rows = rows_f32[slots].reshape((slots.stop - slots.start) * OWN, 2 * DEPTH)
        high = rows.astype(jnp.bfloat16)
        rows_high[part, :] = high
        rows_low[part, :] = (rows - high.astype(jnp.float32)).astype(jnp.bfloat16)

    def product(part, block):
        block_high = block.astype(jnp.bfloat16)
        block_low = (block - block_high.astype(jnp.float32)).astype(jnp.bfloat16)
        value = jnp.dot(rows_high[part, :], block_high, preferred_element_type=jnp.float32)
        value += jnp.dot(rows_low[part, :], block_high, preferred_element_type=jnp.float32)
        value += jnp.dot(rows_high[part, :], block_low, preferred_element_type=jnp.float32)
        return value

    def deliver(group, src, dst, who):
        for dy, dc in who:
            there = (4 - dy) % 4 if dc == 0 else dy
            index = there * 2 + dc - 1
            k = SLOT[dy, dc]
            send(src(pl.ds(k * TILES, TILES)), dst, out_s.at[group, index], out_r.at[group, index], device(dy=dy, dc=dc))

    def own_plane(group, hh, part, who):
        prod[0, part_tiles(part), hh] = tiles_of(product(part, cols[z, hh]))
        deliver(group, lambda t: prod.at[0, t, hh], out_ref.at[:, y, z, hh, c], who)

    def plane_near(group, hh):
        if group == 0:
            split(slice(0, 4))
        own_plane(group, hh, near_rows, NEAR)

    def plane_far(group, hh):
        if group == 0:
            split(slice(4, 8))
        own_plane(group, hh, far_rows, FAR)
        if group == 0:
            row_ids = lax.broadcasted_iota(jnp.int32, (TILES, 8, WIDTH), 0) * 8 + xl * OWN
            row_ids += lax.broadcasted_iota(jnp.int32, (TILES, 8, WIDTH), 1)
            col_ids = lax.broadcasted_iota(jnp.int32, (TILES, 8, WIDTH), 2)
            factor = jnp.where(row_ids == col_ids, jnp.float32(1.0 + damping), jnp.float32(1.0))
            out_ref[:, y, z, hh, c] = prod[0, mine, hh] * factor
        else:
            out_ref[:, y, z, hh, c] = prod[0, mine, hh]

    def mirror_send(d):
        k, (there, _) = MIRRORED.index(d), device(dz=d)
        turned_out[k] = prod[UNITS.index(d) + 1, : 6 * TILES, xh].reshape(6 * OWN, WIDTH).T
        for far, xx in ((0, xl), (1, 1 - xl)):
            src = turned_out.at[k, pl.ds(pl.multiple_of(xx * OWN, 8), OWN), :]
            send(src, turned_in.at[k, xl], mirror_s.at[k, far], mirror_r.at[k, far], (there, xx))

    def mirror_arrived(d):
        k, zz = MIRRORED.index(d), origin(-d)
        for far, xx in ((0, xl), (1, 1 - xl)):
            arrived(turned_in.at[k, xx], mirror_r.at[k, far], mirror_s.at[k, far])
        for (dy, dc), slot in SLOT.items():
            if dy:
                part = slice(slot * OWN, (slot + 1) * OWN)
                strip = jnp.concatenate([turned_in[k, 0][:, part], turned_in[k, 1][:, part]], axis=1)
                out_ref[:, (y + dy * way + NY) % NY, zz, xh, (c + dc) % NC] = tiles_of(strip)

    def multiply(d):
        unit, zz = UNITS.index(d) + 1, origin(d)
        value = product(pl.ds(0, 8 * OWN), jnp.concatenate([cols[zz, 0], cols[zz, 1]], axis=1))
        prod[unit, :, 0] = tiles_of(value[:, :WIDTH])
        prod[unit, :, 1] = tiles_of(value[:, WIDTH:])
        if d in MIRRORED:
            deliver(unit, lambda t: prod.at[unit, t, 1 - xh], out_ref.at[:, y, zz, 1 - xh, c], NEAR + FAR[:2])
            deliver(unit, lambda t: prod.at[unit, t], out_ref.at[:, y, zz, :, c], FAR[2:])
        else:
            deliver(unit, lambda t: prod.at[unit, t], out_ref.at[:, y, zz, :, c], NEAR + FAR)
        out_ref[:, y, zz, 0, c] = prod[unit, mine, 0]
        out_ref[:, y, zz, 1, c] = prod[unit, mine, 1]

    def ring_start(dx, part):
        send(part, part, zl_s.at[0, dx], zl_r.at[0, dx], up)
        send(part, part, zs_s.at[0, dx], zs_r.at[0, dx], down)

    def ring_up(d, dx):
        part = piece(0, origin(-d)) if isinstance(dx, int) and dx == 0 else first(dx, origin(-d))
        arrived(part, zl_r.at[d - 1, dx], zl_s.at[d - 1, dx])
        if d < 4:
            send(part, part, zl_s.at[d, dx], zl_r.at[d, dx], up)

    def ring_down(d, dx):
        part = piece(0, origin(d)) if isinstance(dx, int) and dx == 0 else first(dx, origin(d))
        arrived(part, zs_r.at[d - 1, dx], zs_s.at[d - 1, dx])
        if d < 3:
            send(part, part, zs_s.at[d, dx], zs_r.at[d, dx], down)

    def spread(d):
        part, unit = rest(0, origin(d)), UNITS.index(d)
        for to, there in ((1, 3), (-1, 1)):
            send(part, part, xb_s.at[unit, there - 1], xb_r.at[unit, there - 1], device(dx=to))
        if d in DIRECT:
            send(part, part, xb_s.at[unit, 1], xb_r.at[unit, 1], device(dx=2))

    def spread_came(d, dx):
        part, unit = rest(dx, origin(d)), UNITS.index(d)
        arrived(part, xb_r.at[unit, dx - 1], xb_s.at[unit, dx - 1])
        if dx == 3 and d not in DIRECT:
            send(part, part, xb_s.at[unit, 1], xb_r.at[unit, 1], device(dx=1))

    give_rows(0, half)
    for part, s_sem, r_sem in ((first(0, z), xa_s, xa_r), (rest(0, z), xf_s, xf_r)):
        send(part, part, s_sem.at[1 + towards], r_sem.at[1 + towards], device(dx=towards))
        if s_sem is xa_s:
            ring_start(0, piece(0, z))
        send(part, part, s_sem.at[1 - towards], r_sem.at[1 - towards], device(dx=-towards))
        send(part, part, s_sem.at[1], r_sem.at[1], device(dx=2))

    for event in ORDER:
        kind, at = event[0], event[1:]
        if kind == "swap":
            arrived(rows_f32.at[SLOT[0, 0], :, other_half], swap_r.at[0], swap_s.at[0])
            give_rows(1, other_half)
            pass_rows(0)
        elif kind == "rows":
            rows_arrived(at[0], (half, other_half)[at[0]], at[1])
            if at[0] == 1:
                pass_rows(at[1])
        elif kind == "passed":
            passed(at[0])
        elif kind in ("first", "rest"):
            dx = {"across": across, "beyond": beyond, "opposite": 2}[at[0]]
            if kind == "first":
                arrived(first(dx, z), xa_r.at[dx - 1], xa_s.at[dx - 1])
                ring_start(dx, first(dx, z))
            else:
                arrived(rest(dx, z), xf_r.at[dx - 1], xf_s.at[dx - 1])
        elif kind in ("up", "down"):
            dx = {"own": 0, "across": across, "beyond": beyond, "opposite": 2}[at[1]]
            (ring_up if kind == "up" else ring_down)(at[0], dx)
            if at[1] == "own":
                spread(-at[0] if kind == "up" else at[0])
        elif kind == "spread":
            spread_came(at[0], at[1])
        elif kind == "mirror_send":
            mirror_send(at[0])
        elif kind == "mirror":
            mirror_arrived(at[0])
        elif kind == "near":
            plane_near(at[0], xh if at[0] == 0 else 1 - xh)
        elif kind == "far":
            plane_far(at[0], xh if at[0] == 0 else 1 - xh)
        else:
            multiply(at[0])

    last = len(NEAR + FAR)
    for copy in sends[:-last]:
        copy.wait_send()
    for group, d in ((0, 0), (8, 0), *((unit + 1, d) for unit, d in enumerate(UNITS))):
        for dy, dc in NEAR + FAR:
            index = dy * 2 + dc - 1
            yy, cc = (y + dy * way + NY) % NY, (c + dc) % NC
            zz = (z + d * (1 - 2 * cc) + NZ) % NZ
            if d == 0:
                part = out_ref.at[:, yy, z, xh if group == 0 else 1 - xh, cc]
            elif dy and d in MIRRORED:
                part = out_ref.at[:, yy, zz, 1 - xh, cc]
            else:
                part = out_ref.at[:, yy, zz, :, cc]
            arrived(part, out_r.at[group, index], out_s.at[group, index])
    for copy in sends[-last:]:
        copy.wait_send()


def per_device(jacobian):
    dma = pltpu.SemaphoreType.DMA
    tiles = pl.pallas_call(
        kernel,
        name="gather_multiply_scatter",
        out_shape=jax.ShapeDtypeStruct((TILES, NY, NZ, 2, NC, 8, WIDTH), jnp.float32),
        in_specs=[pl.BlockSpec(memory_space=pltpu.HBM)],
        out_specs=pl.BlockSpec(memory_space=pltpu.VMEM),
        scratch_shapes=[
            pltpu.VMEM((DEPTH, WIDTH), jnp.float32),
            pltpu.VMEM((WIDTH, DEPTH), jnp.float32),
            pltpu.VMEM((NY * NC, OWN, 2 * DEPTH), jnp.float32),
            pltpu.VMEM((NY * NC * OWN, 2 * DEPTH), jnp.bfloat16),
            pltpu.VMEM((NY * NC * OWN, 2 * DEPTH), jnp.bfloat16),
            pltpu.VMEM((NZ, 2, 2 * DEPTH, WIDTH), jnp.float32),
            pltpu.VMEM((NZ, NY * NC * TILES, 2, 8, WIDTH), jnp.float32),
            dma,
            dma((1,)),
            dma((1,)),
            dma((2, 3)),
            dma((2, 3)),
            dma((4,)),
            dma((4,)),
            dma((3,)),
            dma((3,)),
            dma((3,)),
            dma((3,)),
            dma((4, 4)),
            dma((4, 4)),
            dma((3, 4)),
            dma((3, 4)),
            dma((7, 3)),
            dma((7, 3)),
            dma((9, 7)),
            dma((9, 7)),
            pltpu.VMEM((len(MIRRORED), WIDTH, 6 * OWN), jnp.float32),
            pltpu.VMEM((len(MIRRORED), 2, OWN, 6 * OWN), jnp.float32),
            dma((len(MIRRORED), 2)),
            dma((len(MIRRORED), 2)),
        ],
        compiler_params=pltpu.CompilerParams(
            collective_id=0, has_side_effects=True, vmem_limit_bytes=48 * 2**20
        ),
    )(pltpu.with_memory_space_constraint(jacobian, pltpu.HBM))
    tiles = tiles.reshape(TILES, NY * NZ * 2 * NC, 8, WIDTH)
    return jnp.transpose(tiles, (0, 2, 1, 3)).reshape(OWN, NY * NZ * 2 * NC * WIDTH)


def solution(mesh):
    return jax.shard_map(
        per_device,
        mesh=mesh,
        in_specs=(P("grp", "loop"),),
        out_specs=P(("loop", "grp"), None),
        check_vma=False,
    )
```

```python
import jax
import jax.numpy as jnp
from jax import lax
from jax.experimental import pallas as pl
from jax.experimental.pallas import tpu as pltpu
from jax.sharding import PartitionSpec as P

damping = 0.1
MESH = pl.DeviceIdType.MESH
NX, NY, NZ, NC = 4, 4, 8, 2
DEPTH, WIDTH, OWN = 384, 128, 64
TILES = OWN // 8
FIRST = 176


SLOT = {(1, 0): 0, (3, 0): 1, (1, 1): 2, (3, 1): 3, (2, 0): 4, (2, 1): 5, (0, 0): 6, (0, 1): 7}
NEAR, FAR = ((1, 0), (3, 0), (1, 1), (3, 1)), ((2, 0), (2, 1), (0, 1))
UNITS = (-1, 1, -2, 2, -3, 3, -4)
MIRRORED = (-1, 1)
DIRECT = (-1, 1, -2, 2, -3, 3, -4)
ORDER = (
    ("swap",),
    ("rows", 0, 3),
    ("first", "across"),
    ("rows", 0, 1),
    ("up", 1, "own"),
    ("passed", 0),
    ("first", "beyond"),
    ("rows", 1, 3),
    ("rows", 1, 1),
    ("down", 1, "own"),
    ("passed", 1),
    ("first", "opposite"),
    ("rows", 0, 2),
    ("up", 1, "across"),
    ("rest", "across"),
    ("passed", 3),
    ("near", 0),
    ("rows", 1, 2),
    ("down", 1, "across"),
    ("rest", "beyond"),
    ("passed", 2),
    ("far", 0),
    ("up", 2, "own"),
    ("up", 1, "beyond"),
    ("rest", "opposite"),
    ("near", 8),
    ("spread", -1, 3),
    ("far", 8),
    ("down", 1, "beyond"),
    ("spread", -1, 1),
    ("down", 2, "own"),
    ("up", 1, "opposite"),
    ("spread", -1, 2),
    ("multiply", -1),
    ("down", 1, "opposite"),
    ("spread", 1, 3),
    ("up", 2, "across"),
    ("spread", 1, 1),
    ("down", 2, "across"),
    ("up", 3, "own"),
    ("spread", 1, 2),
    ("multiply", 1),
    ("spread", -2, 3),
    ("up", 2, "beyond"),
    ("down", 2, "beyond"),
    ("spread", -2, 1),
    ("down", 3, "own"),
    ("spread", -2, 2),
    ("up", 2, "opposite"),
    ("multiply", -2),
    ("spread", 2, 3),
    ("down", 2, "opposite"),
    ("spread", 2, 1),
    ("up", 3, "across"),
    ("down", 3, "across"),
    ("spread", 2, 2),
    ("multiply", 2),
    ("spread", -3, 3),
    ("up", 4, "own"),
    ("up", 3, "beyond"),
    ("spread", -3, 1),
    ("down", 3, "beyond"),
    ("up", 3, "opposite"),
    ("down", 3, "opposite"),
    ("spread", -3, 2),
    ("multiply", -3),
    ("spread", 3, 3),
    ("up", 4, "across"),
    ("spread", 3, 1),
    ("up", 4, "beyond"),
    ("up", 4, "opposite"),
    ("spread", 3, 2),
    ("multiply", 3),
    ("mirror_send", -1),
    ("mirror_send", 1),
    ("spread", -4, 3),
    ("spread", -4, 1),
    ("spread", -4, 2),
    ("multiply", -4),
    ("mirror", -1),
    ("mirror", 1),
)


def kernel(
    a_ref,
    out_ref,
    own,
    turned,
    rows_f32,
    rows_high,
    rows_low,
    cols,
    prod,
    own_sem,
    swap_s,
    swap_r,
    row_s,
    row_r,
    pass_s,
    pass_r,
    xa_s,
    xa_r,
    xf_s,
    xf_r,
    zl_s,
    zl_r,
    zs_s,
    zs_r,
    xb_s,
    xb_r,
    out_s,
    out_r,
    turned_out,
    turned_in,
    mirror_s,
    mirror_r,
):
    loop, xl = lax.axis_index("loop"), lax.axis_index("grp")
    c = loop % 2
    xh = (loop // 2) % 2
    z = (loop // 4) % NZ
    y = loop // 32
    x = xh * 2 + xl
    way = 1 - 2 * c

    def device(dx=0, dy=0, dz=0, dc=0):
        xx, yy, zz = (x + dx * way + NX) % NX, (y + dy * way + NY) % NY, (z + dz * way + NZ) % NZ
        return ((yy * NZ + zz) * 2 + xx // 2) * 2 + (c + dc) % NC, xx % 2

    sends = []

    def send(src, dst, s_sem, r_sem, to):
        copy = pltpu.make_async_remote_copy(
            src_ref=src, dst_ref=dst, send_sem=s_sem, recv_sem=r_sem, device_id=to, device_id_type=MESH
        )
        copy.start()
        sends.append(copy)

    mate = (loop, 1 - xl)

    def arrived(ref, r_sem, s_sem):
        pltpu.make_async_remote_copy(
            src_ref=ref, dst_ref=ref, send_sem=s_sem, recv_sem=r_sem, device_id=mate, device_id_type=MESH
        ).wait_recv()

    def piece(dx, zz, start=0, size=DEPTH):
        xx = (x + dx * way + NX) % NX
        return cols.at[zz, xx // 2, pl.ds(pl.multiple_of((xx % 2) * DEPTH + start, 8), size), :]

    def first(dx, zz):
        return piece(dx, zz, 0, FIRST)

    def rest(dx, zz):
        return piece(dx, zz, FIRST, DEPTH - FIRST)

    def origin(d):
        return (z + d * way + NZ) % NZ

    half = pl.ds(pl.multiple_of(xl * DEPTH, 128), DEPTH)
    other_half = pl.ds(pl.multiple_of((1 - xl) * DEPTH, 128), DEPTH)

    load = pltpu.make_async_copy(a_ref, own, own_sem)
    load.start()
    barrier = pltpu.get_barrier_semaphore()
    greeted = [device(dx=d) for d in (1, 2, 3)] + [device(dz=1), device(dz=-1), device(dc=1)]
    greeted += [device(dy=d, dc=e) for d in (1, 2, 3) for e in (0, 1)]
    greeted += [(device(dz=d)[0], 1 - xl) for d in (1, -1)]
    for who in greeted:
        pl.semaphore_signal(barrier, inc=1, device_id=who, device_id_type=MESH)
    load.wait()
    block = own[...]
    turned[...] = block.T
    rows_f32[SLOT[0, 0], :, half] = turned[pl.ds(pl.multiple_of(xl * OWN, 8), OWN), :]
    cols[z, xh, pl.ds(pl.multiple_of(xl * DEPTH, 8), DEPTH), :] = block
    pl.semaphore_wait(barrier, len(greeted))

    send(
        turned.at[pl.ds(pl.multiple_of((1 - xl) * OWN, 8), OWN), :],
        rows_f32.at[SLOT[0, 0], :, half],
        swap_s.at[0],
        swap_r.at[0],
        mate,
    )

    def give_rows(part, lanes):
        for to, there in ((1, 3), (-1, 1), (2, 2)):
            send(
                rows_f32.at[SLOT[0, 0], :, lanes],
                rows_f32.at[SLOT[there, 0], :, lanes],
                row_s.at[part, there - 1],
                row_r.at[part, there - 1],
                device(dy=to),
            )

    def rows_arrived(part, lanes, dy):
        slot = rows_f32.at[SLOT[dy, 0], :, lanes]
        arrived(slot, row_r.at[part, dy - 1], row_s.at[part, dy - 1])

    def pass_rows(dy):
        send(
            rows_f32.at[SLOT[dy, 0]],
            rows_f32.at[SLOT[(4 - dy) % 4, 1]],
            pass_s.at[(4 - dy) % 4],
            pass_r.at[(4 - dy) % 4],
            device(dc=1),
        )

    def passed(dy):
        arrived(rows_f32.at[SLOT[dy, 1]], pass_r.at[dy], pass_s.at[dy])

    towards = (1 - 2 * xl) * way
    across, beyond = (towards + NX) % NX, (NX - towards) % NX
    up, down = device(dz=1), device(dz=-1)
    near_rows, far_rows = pl.ds(0, 4 * OWN), pl.ds(4 * OWN, 4 * OWN)
    mine = pl.ds(SLOT[0, 0] * TILES, TILES)

    def part_tiles(part):
        return pl.ds(part.start // 8, part.size // 8)

    def tiles_of(value):
        return value.reshape(value.shape[0] // 8, 8, WIDTH)


    def split(slots):
        part = pl.ds(slots.start * OWN, (slots.stop - slots.start) * OWN)
        rows = rows_f32[slots].reshape((slots.stop - slots.start) * OWN, 2 * DEPTH)
        high = rows.astype(jnp.bfloat16)
        rows_high[part, :] = high
        rows_low[part, :] = (rows - high.astype(jnp.float32)).astype(jnp.bfloat16)

    def product(part, block):
        block_high = block.astype(jnp.bfloat16)
        block_low = (block - block_high.astype(jnp.float32)).astype(jnp.bfloat16)
        value = jnp.dot(rows_high[part, :], block_high, preferred_element_type=jnp.float32)
        value += jnp.dot(rows_low[part, :], block_high, preferred_element_type=jnp.float32)
        value += jnp.dot(rows_high[part, :], block_low, preferred_element_type=jnp.float32)
        return value

    def deliver(group, src, dst, who):
        for dy, dc in who:
            there = (4 - dy) % 4 if dc == 0 else dy
            index = there * 2 + dc - 1
            k = SLOT[dy, dc]
            send(src(pl.ds(k * TILES, TILES)), dst, out_s.at[group, index], out_r.at[group, index], device(dy=dy, dc=dc))

    def own_plane(group, hh, part, who):
        prod[0, part_tiles(part), hh] = tiles_of(product(part, cols[z, hh]))
        deliver(group, lambda t: prod.at[0, t, hh], out_ref.at[:, y, z, hh, c], who)

    def plane_near(group, hh):
        if group == 0:
            split(slice(0, 4))
        own_plane(group, hh, near_rows, NEAR)

    def plane_far(group, hh):
        if group == 0:
            split(slice(4, 8))
        own_plane(group, hh, far_rows, FAR)
        if group == 0:
            row_ids = lax.broadcasted_iota(jnp.int32, (TILES, 8, WIDTH), 0) * 8 + xl * OWN
            row_ids += lax.broadcasted_iota(jnp.int32, (TILES, 8, WIDTH), 1)
            col_ids = lax.broadcasted_iota(jnp.int32, (TILES, 8, WIDTH), 2)
            factor = jnp.where(row_ids == col_ids, jnp.float32(1.0 + damping), jnp.float32(1.0))
            out_ref[:, y, z, hh, c] = prod[0, mine, hh] * factor
        else:
            out_ref[:, y, z, hh, c] = prod[0, mine, hh]

    def mirror_send(d):
        k, (there, _) = MIRRORED.index(d), device(dz=d)
        turned_out[k] = prod[UNITS.index(d) + 1, : 6 * TILES, xh].reshape(6 * OWN, WIDTH).T
        for far, xx in ((0, xl), (1, 1 - xl)):
            src = turned_out.at[k, pl.ds(pl.multiple_of(xx * OWN, 8), OWN), :]
            send(src, turned_in.at[k, xl], mirror_s.at[k, far], mirror_r.at[k, far], (there, xx))

    def mirror_arrived(d):
        k, zz = MIRRORED.index(d), origin(-d)
        for far, xx in ((0, xl), (1, 1 - xl)):
            arrived(turned_in.at[k, xx], mirror_r.at[k, far], mirror_s.at[k, far])
        for (dy, dc), slot in SLOT.items():
            if dy:
                part = slice(slot * OWN, (slot + 1) * OWN)
                strip = jnp.concatenate([turned_in[k, 0][:, part], turned_in[k, 1][:, part]], axis=1)
                out_ref[:, (y + dy * way + NY) % NY, zz, xh, (c + dc) % NC] = tiles_of(strip)

    def multiply(d):
        unit, zz = UNITS.index(d) + 1, origin(d)
        value = product(pl.ds(0, 8 * OWN), jnp.concatenate([cols[zz, 0], cols[zz, 1]], axis=1))
        prod[unit, :, 0] = tiles_of(value[:, :WIDTH])
        prod[unit, :, 1] = tiles_of(value[:, WIDTH:])
        if d in MIRRORED:
            deliver(unit, lambda t: prod.at[unit, t, 1 - xh], out_ref.at[:, y, zz, 1 - xh, c], NEAR + FAR[:2])
            deliver(unit, lambda t: prod.at[unit, t], out_ref.at[:, y, zz, :, c], FAR[2:])
        else:
            deliver(unit, lambda t: prod.at[unit, t], out_ref.at[:, y, zz, :, c], NEAR + FAR)
        out_ref[:, y, zz, 0, c] = prod[unit, mine, 0]
        out_ref[:, y, zz, 1, c] = prod[unit, mine, 1]

    def ring_start(dx, part):
        send(part, part, zl_s.at[0, dx], zl_r.at[0, dx], up)
        send(part, part, zs_s.at[0, dx], zs_r.at[0, dx], down)

    def ring_up(d, dx):
        part = piece(0, origin(-d)) if isinstance(dx, int) and dx == 0 else first(dx, origin(-d))
        arrived(part, zl_r.at[d - 1, dx], zl_s.at[d - 1, dx])
        if d < 4:
            send(part, part, zl_s.at[d, dx], zl_r.at[d, dx], up)

    def ring_down(d, dx):
        part = piece(0, origin(d)) if isinstance(dx, int) and dx == 0 else first(dx, origin(d))
        arrived(part, zs_r.at[d - 1, dx], zs_s.at[d - 1, dx])
        if d < 3:
            send(part, part, zs_s.at[d, dx], zs_r.at[d, dx], down)

    def spread(d):
        part, unit = rest(0, origin(d)), UNITS.index(d)
        for to, there in ((1, 3), (-1, 1)):
            send(part, part, xb_s.at[unit, there - 1], xb_r.at[unit, there - 1], device(dx=to))
        if d in DIRECT:
            send(part, part, xb_s.at[unit, 1], xb_r.at[unit, 1], device(dx=2))

    def spread_came(d, dx):
        part, unit = rest(dx, origin(d)), UNITS.index(d)
        arrived(part, xb_r.at[unit, dx - 1], xb_s.at[unit, dx - 1])
        if dx == 3 and d not in DIRECT:
            send(part, part, xb_s.at[unit, 1], xb_r.at[unit, 1], device(dx=1))

    give_rows(0, half)
    for part, s_sem, r_sem in ((first(0, z), xa_s, xa_r), (rest(0, z), xf_s, xf_r)):
        send(part, part, s_sem.at[1 + towards], r_sem.at[1 + towards], device(dx=towards))
        if s_sem is xa_s:
            ring_start(0, piece(0, z))
        send(part, part, s_sem.at[1 - towards], r_sem.at[1 - towards], device(dx=-towards))
        send(part, part, s_sem.at[1], r_sem.at[1], device(dx=2))

    for event in ORDER:
        kind, at = event[0], event[1:]
        if kind == "swap":
            arrived(rows_f32.at[SLOT[0, 0], :, other_half], swap_r.at[0], swap_s.at[0])
            give_rows(1, other_half)
            pass_rows(0)
        elif kind == "rows":
            rows_arrived(at[0], (half, other_half)[at[0]], at[1])
            if at[0] == 1:
                pass_rows(at[1])
        elif kind == "passed":
            passed(at[0])
        elif kind in ("first", "rest"):
            dx = {"across": across, "beyond": beyond, "opposite": 2}[at[0]]
            if kind == "first":
                arrived(first(dx, z), xa_r.at[dx - 1], xa_s.at[dx - 1])
                ring_start(dx, first(dx, z))
            else:
                arrived(rest(dx, z), xf_r.at[dx - 1], xf_s.at[dx - 1])
        elif kind in ("up", "down"):
            dx = {"own": 0, "across": across, "beyond": beyond, "opposite": 2}[at[1]]
            (ring_up if kind == "up" else ring_down)(at[0], dx)
            if at[1] == "own":
                spread(-at[0] if kind == "up" else at[0])
        elif kind == "spread":
            spread_came(at[0], at[1])
        elif kind == "mirror_send":
            mirror_send(at[0])
        elif kind == "mirror":
            mirror_arrived(at[0])
        elif kind == "near":
            plane_near(at[0], xh if at[0] == 0 else 1 - xh)
        elif kind == "far":
            plane_far(at[0], xh if at[0] == 0 else 1 - xh)
        else:
            multiply(at[0])

    last = len(NEAR + FAR)
    for copy in sends[:-last]:
        copy.wait_send()
    for group, d in ((0, 0), (8, 0), *((unit + 1, d) for unit, d in enumerate(UNITS))):
        for dy, dc in NEAR + FAR:
            index = dy * 2 + dc - 1
            yy, cc = (y + dy * way + NY) % NY, (c + dc) % NC
            zz = (z + d * (1 - 2 * cc) + NZ) % NZ
            if d == 0:
                part = out_ref.at[:, yy, z, xh if group == 0 else 1 - xh, cc]
            elif dy and d in MIRRORED:
                part = out_ref.at[:, yy, zz, 1 - xh, cc]
            else:
                part = out_ref.at[:, yy, zz, :, cc]
            arrived(part, out_r.at[group, index], out_s.at[group, index])
    for copy in sends[-last:]:
        copy.wait_send()


def per_device(jacobian):
    dma = pltpu.SemaphoreType.DMA
    tiles = pl.pallas_call(
        kernel,
        name="gather_multiply_scatter",
        out_shape=jax.ShapeDtypeStruct((TILES, NY, NZ, 2, NC, 8, WIDTH), jnp.float32),
        in_specs=[pl.BlockSpec(memory_space=pltpu.HBM)],
        out_specs=pl.BlockSpec(memory_space=pltpu.VMEM),
        scratch_shapes=[
            pltpu.VMEM((DEPTH, WIDTH), jnp.float32),
            pltpu.VMEM((WIDTH, DEPTH), jnp.float32),
            pltpu.VMEM((NY * NC, OWN, 2 * DEPTH), jnp.float32),
            pltpu.VMEM((NY * NC * OWN, 2 * DEPTH), jnp.bfloat16),
            pltpu.VMEM((NY * NC * OWN, 2 * DEPTH), jnp.bfloat16),
            pltpu.VMEM((NZ, 2, 2 * DEPTH, WIDTH), jnp.float32),
            pltpu.VMEM((NZ, NY * NC * TILES, 2, 8, WIDTH), jnp.float32),
            dma,
            dma((1,)),
            dma((1,)),
            dma((2, 3)),
            dma((2, 3)),
            dma((4,)),
            dma((4,)),
            dma((3,)),
            dma((3,)),
            dma((3,)),
            dma((3,)),
            dma((4, 4)),
            dma((4, 4)),
            dma((3, 4)),
            dma((3, 4)),
            dma((7, 3)),
            dma((7, 3)),
            dma((9, 7)),
            dma((9, 7)),
            pltpu.VMEM((len(MIRRORED), WIDTH, 6 * OWN), jnp.float32),
            pltpu.VMEM((len(MIRRORED), 2, OWN, 6 * OWN), jnp.float32),
            dma((len(MIRRORED), 2)),
            dma((len(MIRRORED), 2)),
        ],
        compiler_params=pltpu.CompilerParams(
            collective_id=0, has_side_effects=True, vmem_limit_bytes=48 * 2**20
        ),
    )(pltpu.with_memory_space_constraint(jacobian, pltpu.HBM))
    tiles = tiles.reshape(TILES, NY * NZ * 2 * NC, 8, WIDTH)
    return jnp.transpose(tiles, (0, 2, 1, 3)).reshape(OWN, NY * NZ * 2 * NC * WIDTH)


def solution(mesh):
    return jax.shard_map(
        per_device,
        mesh=mesh,
        in_specs=(P("grp", "loop"),),
        out_specs=P(("loop", "grp"), None),
        check_vma=False,
    )
```

```python
import jax
import jax.numpy as jnp
from jax import lax
from jax.experimental import pallas as pl
from jax.experimental.pallas import tpu as pltpu
from jax.sharding import PartitionSpec as P

damping = 0.1
MESH = pl.DeviceIdType.MESH
NX, NY, NZ, NC = 4, 4, 8, 2
DEPTH, WIDTH, OWN = 384, 128, 64
TILES = OWN // 8
FIRST = 176


SLOT = {(1, 0): 0, (3, 0): 1, (1, 1): 2, (3, 1): 3, (2, 0): 4, (2, 1): 5, (0, 0): 6, (0, 1): 7}
NEAR, FAR = ((1, 0), (3, 0), (1, 1), (3, 1)), ((2, 0), (2, 1), (0, 1))
UNITS = (-1, 1, -2, 2, -3, 3, -4)
MIRRORED = (-1, 1)
DIRECT = (-1, 1, -2, 2, -3, 3)
ORDER = (
    ("swap",),
    ("rows", 0, 3),
    ("first", "across"),
    ("rows", 0, 1),
    ("up", 1, "own"),
    ("passed", 0),
    ("first", "beyond"),
    ("rows", 1, 3),
    ("rows", 1, 1),
    ("down", 1, "own"),
    ("passed", 1),
    ("first", "opposite"),
    ("rows", 0, 2),
    ("up", 1, "across"),
    ("rest", "across"),
    ("passed", 3),
    ("near", 0),
    ("rows", 1, 2),
    ("down", 1, "across"),
    ("rest", "beyond"),
    ("passed", 2),
    ("far", 0),
    ("up", 2, "own"),
    ("up", 1, "beyond"),
    ("rest", "opposite"),
    ("near", 8),
    ("spread", -1, 3),
    ("far", 8),
    ("down", 1, "beyond"),
    ("spread", -1, 1),
    ("down", 2, "own"),
    ("up", 1, "opposite"),
    ("spread", -1, 2),
    ("multiply", -1),
    ("down", 1, "opposite"),
    ("spread", 1, 3),
    ("up", 2, "across"),
    ("spread", 1, 1),
    ("down", 2, "across"),
    ("up", 3, "own"),
    ("spread", 1, 2),
    ("multiply", 1),
    ("spread", -2, 3),
    ("up", 2, "beyond"),
    ("down", 2, "beyond"),
    ("spread", -2, 1),
    ("down", 3, "own"),
    ("spread", -2, 2),
    ("up", 2, "opposite"),
    ("multiply", -2),
    ("spread", 2, 3),
    ("down", 2, "opposite"),
    ("spread", 2, 1),
    ("up", 3, "across"),
    ("down", 3, "across"),
    ("spread", 2, 2),
    ("multiply", 2),
    ("spread", -3, 3),
    ("up", 4, "own"),
    ("up", 3, "beyond"),
    ("spread", -3, 1),
    ("down", 3, "beyond"),
    ("up", 3, "opposite"),
    ("down", 3, "opposite"),
    ("spread", -3, 2),
    ("multiply", -3),
    ("spread", 3, 3),
    ("up", 4, "across"),
    ("spread", 3, 1),
    ("up", 4, "beyond"),
    ("up", 4, "opposite"),
    ("spread", 3, 2),
    ("multiply", 3),
    ("mirror_send", -1),
    ("mirror_send", 1),
    ("spread", -4, 3),
    ("spread", -4, 1),
    ("spread", -4, 2),
    ("multiply", -4),
    ("mirror", -1),
    ("mirror", 1),
)


def kernel(
    a_ref,
    out_ref,
    own,
    turned,
    rows_f32,
    rows_high,
    rows_low,
    cols,
    prod,
    own_sem,
    swap_s,
    swap_r,
    row_s,
    row_r,
    pass_s,
    pass_r,
    xa_s,
    xa_r,
    xf_s,
    xf_r,
    zl_s,
    zl_r,
    zs_s,
    zs_r,
    xb_s,
    xb_r,
    out_s,
    out_r,
    turned_out,
    turned_in,
    mirror_s,
    mirror_r,
):
    loop, xl = lax.axis_index("loop"), lax.axis_index("grp")
    c = loop % 2
    xh = (loop // 2) % 2
    z = (loop // 4) % NZ
    y = loop // 32
    x = xh * 2 + xl
    way = 1 - 2 * c

    def device(dx=0, dy=0, dz=0, dc=0):
        xx, yy, zz = (x + dx * way + NX) % NX, (y + dy * way + NY) % NY, (z + dz * way + NZ) % NZ
        return ((yy * NZ + zz) * 2 + xx // 2) * 2 + (c + dc) % NC, xx % 2

    sends = []

    def send(src, dst, s_sem, r_sem, to):
        copy = pltpu.make_async_remote_copy(
            src_ref=src, dst_ref=dst, send_sem=s_sem, recv_sem=r_sem, device_id=to, device_id_type=MESH
        )
        copy.start()
        sends.append(copy)

    mate = (loop, 1 - xl)

    def arrived(ref, r_sem, s_sem):
        pltpu.make_async_remote_copy(
            src_ref=ref, dst_ref=ref, send_sem=s_sem, recv_sem=r_sem, device_id=mate, device_id_type=MESH
        ).wait_recv()

    def piece(dx, zz, start=0, size=DEPTH):
        xx = (x + dx * way + NX) % NX
        return cols.at[zz, xx // 2, pl.ds(pl.multiple_of((xx % 2) * DEPTH + start, 8), size), :]

    def first(dx, zz):
        return piece(dx, zz, 0, FIRST)

    def rest(dx, zz):
        return piece(dx, zz, FIRST, DEPTH - FIRST)

    def origin(d):
        return (z + d * way + NZ) % NZ

    half = pl.ds(pl.multiple_of(xl * DEPTH, 128), DEPTH)
    other_half = pl.ds(pl.multiple_of((1 - xl) * DEPTH, 128), DEPTH)

    load = pltpu.make_async_copy(a_ref, own, own_sem)
    load.start()
    barrier = pltpu.get_barrier_semaphore()
    greeted = [device(dx=d) for d in (1, 2, 3)] + [device(dz=1), device(dz=-1), device(dc=1)]
    greeted += [device(dy=d, dc=e) for d in (1, 2, 3) for e in (0, 1)]
    greeted += [(device(dz=d)[0], 1 - xl) for d in (1, -1)]
    for who in greeted:
        pl.semaphore_signal(barrier, inc=1, device_id=who, device_id_type=MESH)
    load.wait()
    block = own[...]
    turned[...] = block.T
    rows_f32[SLOT[0, 0], :, half] = turned[pl.ds(pl.multiple_of(xl * OWN, 8), OWN), :]
    cols[z, xh, pl.ds(pl.multiple_of(xl * DEPTH, 8), DEPTH), :] = block
    pl.semaphore_wait(barrier, len(greeted))

    send(
        turned.at[pl.ds(pl.multiple_of((1 - xl) * OWN, 8), OWN), :],
        rows_f32.at[SLOT[0, 0], :, half],
        swap_s.at[0],
        swap_r.at[0],
        mate,
    )

    def give_rows(part, lanes):
        for to, there in ((1, 3), (-1, 1), (2, 2)):
            send(
                rows_f32.at[SLOT[0, 0], :, lanes],
                rows_f32.at[SLOT[there, 0], :, lanes],
                row_s.at[part, there - 1],
                row_r.at[part, there - 1],
                device(dy=to),
            )

    def rows_arrived(part, lanes, dy):
        slot = rows_f32.at[SLOT[dy, 0], :, lanes]
        arrived(slot, row_r.at[part, dy - 1], row_s.at[part, dy - 1])

    def pass_rows(dy):
        send(
            rows_f32.at[SLOT[dy, 0]],
            rows_f32.at[SLOT[(4 - dy) % 4, 1]],
            pass_s.at[(4 - dy) % 4],
            pass_r.at[(4 - dy) % 4],
            device(dc=1),
        )

    def passed(dy):
        arrived(rows_f32.at[SLOT[dy, 1]], pass_r.at[dy], pass_s.at[dy])

    towards = (1 - 2 * xl) * way
    across, beyond = (towards + NX) % NX, (NX - towards) % NX
    up, down = device(dz=1), device(dz=-1)
    near_rows, far_rows = pl.ds(0, 4 * OWN), pl.ds(4 * OWN, 4 * OWN)
    mine = pl.ds(SLOT[0, 0] * TILES, TILES)

    def part_tiles(part):
        return pl.ds(part.start // 8, part.size // 8)

    def tiles_of(value):
        return value.reshape(value.shape[0] // 8, 8, WIDTH)


    def split(slots):
        part = pl.ds(slots.start * OWN, (slots.stop - slots.start) * OWN)
        rows = rows_f32[slots].reshape((slots.stop - slots.start) * OWN, 2 * DEPTH)
        high = rows.astype(jnp.bfloat16)
        rows_high[part, :] = high
        rows_low[part, :] = (rows - high.astype(jnp.float32)).astype(jnp.bfloat16)

    def product(part, block):
        block_high = block.astype(jnp.bfloat16)
        block_low = (block - block_high.astype(jnp.float32)).astype(jnp.bfloat16)
        value = jnp.dot(rows_high[part, :], block_high, preferred_element_type=jnp.float32)
        value += jnp.dot(rows_low[part, :], block_high, preferred_element_type=jnp.float32)
        value += jnp.dot(rows_high[part, :], block_low, preferred_element_type=jnp.float32)
        return value

    def deliver(group, src, dst, who):
        for dy, dc in who:
            there = (4 - dy) % 4 if dc == 0 else dy
            index = there * 2 + dc - 1
            k = SLOT[dy, dc]
            send(src(pl.ds(k * TILES, TILES)), dst, out_s.at[group, index], out_r.at[group, index], device(dy=dy, dc=dc))

    def own_plane(group, hh, part, who):
        prod[0, part_tiles(part), hh] = tiles_of(product(part, cols[z, hh]))
        deliver(group, lambda t: prod.at[0, t, hh], out_ref.at[:, y, z, hh, c], who)

    def plane_near(group, hh):
        if group == 0:
            split(slice(0, 4))
        own_plane(group, hh, near_rows, NEAR)

    def plane_far(group, hh):
        if group == 0:
            split(slice(4, 8))
        own_plane(group, hh, far_rows, FAR)
        if group == 0:
            row_ids = lax.broadcasted_iota(jnp.int32, (TILES, 8, WIDTH), 0) * 8 + xl * OWN
            row_ids += lax.broadcasted_iota(jnp.int32, (TILES, 8, WIDTH), 1)
            col_ids = lax.broadcasted_iota(jnp.int32, (TILES, 8, WIDTH), 2)
            factor = jnp.where(row_ids == col_ids, jnp.float32(1.0 + damping), jnp.float32(1.0))
            out_ref[:, y, z, hh, c] = prod[0, mine, hh] * factor
        else:
            out_ref[:, y, z, hh, c] = prod[0, mine, hh]

    def mirror_send(d):
        k, (there, _) = MIRRORED.index(d), device(dz=d)
        turned_out[k] = prod[UNITS.index(d) + 1, : 6 * TILES, xh].reshape(6 * OWN, WIDTH).T
        for far, xx in ((0, xl), (1, 1 - xl)):
            src = turned_out.at[k, pl.ds(pl.multiple_of(xx * OWN, 8), OWN), :]
            send(src, turned_in.at[k, xl], mirror_s.at[k, far], mirror_r.at[k, far], (there, xx))

    def mirror_arrived(d):
        k, zz = MIRRORED.index(d), origin(-d)
        for far, xx in ((0, xl), (1, 1 - xl)):
            arrived(turned_in.at[k, xx], mirror_r.at[k, far], mirror_s.at[k, far])
        for (dy, dc), slot in SLOT.items():
            if dy:
                part = slice(slot * OWN, (slot + 1) * OWN)
                strip = jnp.concatenate([turned_in[k, 0][:, part], turned_in[k, 1][:, part]], axis=1)
                out_ref[:, (y + dy * way + NY) % NY, zz, xh, (c + dc) % NC] = tiles_of(strip)

    def multiply(d):
        unit, zz = UNITS.index(d) + 1, origin(d)
        value = product(pl.ds(0, 8 * OWN), jnp.concatenate([cols[zz, 0], cols[zz, 1]], axis=1))
        prod[unit, :, 0] = tiles_of(value[:, :WIDTH])
        prod[unit, :, 1] = tiles_of(value[:, WIDTH:])
        if d in MIRRORED:
            deliver(unit, lambda t: prod.at[unit, t, 1 - xh], out_ref.at[:, y, zz, 1 - xh, c], NEAR + FAR[:2])
            deliver(unit, lambda t: prod.at[unit, t], out_ref.at[:, y, zz, :, c], FAR[2:])
        else:
            deliver(unit, lambda t: prod.at[unit, t], out_ref.at[:, y, zz, :, c], FAR + NEAR)
        out_ref[:, y, zz, 0, c] = prod[unit, mine, 0]
        out_ref[:, y, zz, 1, c] = prod[unit, mine, 1]

    def ring_start(dx, part):
        send(part, part, zl_s.at[0, dx], zl_r.at[0, dx], up)
        send(part, part, zs_s.at[0, dx], zs_r.at[0, dx], down)

    def ring_up(d, dx):
        part = piece(0, origin(-d)) if isinstance(dx, int) and dx == 0 else first(dx, origin(-d))
        arrived(part, zl_r.at[d - 1, dx], zl_s.at[d - 1, dx])
        if d < 4:
            send(part, part, zl_s.at[d, dx], zl_r.at[d, dx], up)

    def ring_down(d, dx):
        part = piece(0, origin(d)) if isinstance(dx, int) and dx == 0 else first(dx, origin(d))
        arrived(part, zs_r.at[d - 1, dx], zs_s.at[d - 1, dx])
        if d < 3:
            send(part, part, zs_s.at[d, dx], zs_r.at[d, dx], down)

    def spread(d):
        part, unit = rest(0, origin(d)), UNITS.index(d)
        for to, there in ((1, 3), (-1, 1)):
            send(part, part, xb_s.at[unit, there - 1], xb_r.at[unit, there - 1], device(dx=to))
        if d in DIRECT:
            send(part, part, xb_s.at[unit, 1], xb_r.at[unit, 1], device(dx=2))

    def spread_came(d, dx):
        part, unit = rest(dx, origin(d)), UNITS.index(d)
        arrived(part, xb_r.at[unit, dx - 1], xb_s.at[unit, dx - 1])
        if dx == 3 and d not in DIRECT:
            send(part, part, xb_s.at[unit, 1], xb_r.at[unit, 1], device(dx=1))

    give_rows(0, half)
    for part, s_sem, r_sem in ((first(0, z), xa_s, xa_r), (rest(0, z), xf_s, xf_r)):
        send(part, part, s_sem.at[1 + towards], r_sem.at[1 + towards], device(dx=towards))
        if s_sem is xa_s:
            ring_start(0, piece(0, z))
        send(part, part, s_sem.at[1 - towards], r_sem.at[1 - towards], device(dx=-towards))
        send(part, part, s_sem.at[1], r_sem.at[1], device(dx=2))

    for event in ORDER:
        kind, at = event[0], event[1:]
        if kind == "swap":
            arrived(rows_f32.at[SLOT[0, 0], :, other_half], swap_r.at[0], swap_s.at[0])
            give_rows(1, other_half)
            pass_rows(0)
        elif kind == "rows":
            rows_arrived(at[0], (half, other_half)[at[0]], at[1])
            if at[0] == 1:
                pass_rows(at[1])
        elif kind == "passed":
            passed(at[0])
        elif kind in ("first", "rest"):
            dx = {"across": across, "beyond": beyond, "opposite": 2}[at[0]]
            if kind == "first":
                arrived(first(dx, z), xa_r.at[dx - 1], xa_s.at[dx - 1])
                ring_start(dx, first(dx, z))
            else:
                arrived(rest(dx, z), xf_r.at[dx - 1], xf_s.at[dx - 1])
        elif kind in ("up", "down"):
            dx = {"own": 0, "across": across, "beyond": beyond, "opposite": 2}[at[1]]
            (ring_up if kind == "up" else ring_down)(at[0], dx)
            if at[1] == "own":
                spread(-at[0] if kind == "up" else at[0])
        elif kind == "spread":
            spread_came(at[0], at[1])
        elif kind == "mirror_send":
            mirror_send(at[0])
        elif kind == "mirror":
            mirror_arrived(at[0])
        elif kind == "near":
            plane_near(at[0], xh if at[0] == 0 else 1 - xh)
        elif kind == "far":
            plane_far(at[0], xh if at[0] == 0 else 1 - xh)
        else:
            multiply(at[0])

    last = len(NEAR + FAR)
    for copy in sends[:-last]:
        copy.wait_send()
    for group, d in ((0, 0), (8, 0), *((unit + 1, d) for unit, d in enumerate(UNITS))):
        for dy, dc in NEAR + FAR:
            index = dy * 2 + dc - 1
            yy, cc = (y + dy * way + NY) % NY, (c + dc) % NC
            zz = (z + d * (1 - 2 * cc) + NZ) % NZ
            if d == 0:
                part = out_ref.at[:, yy, z, xh if group == 0 else 1 - xh, cc]
            elif dy and d in MIRRORED:
                part = out_ref.at[:, yy, zz, 1 - xh, cc]
            else:
                part = out_ref.at[:, yy, zz, :, cc]
            arrived(part, out_r.at[group, index], out_s.at[group, index])
    for copy in sends[-last:]:
        copy.wait_send()


def per_device(jacobian):
    dma = pltpu.SemaphoreType.DMA
    tiles = pl.pallas_call(
        kernel,
        name="gather_multiply_scatter",
        out_shape=jax.ShapeDtypeStruct((TILES, NY, NZ, 2, NC, 8, WIDTH), jnp.float32),
        in_specs=[pl.BlockSpec(memory_space=pltpu.HBM)],
        out_specs=pl.BlockSpec(memory_space=pltpu.VMEM),
        scratch_shapes=[
            pltpu.VMEM((DEPTH, WIDTH), jnp.float32),
            pltpu.VMEM((WIDTH, DEPTH), jnp.float32),
            pltpu.VMEM((NY * NC, OWN, 2 * DEPTH), jnp.float32),
            pltpu.VMEM((NY * NC * OWN, 2 * DEPTH), jnp.bfloat16),
            pltpu.VMEM((NY * NC * OWN, 2 * DEPTH), jnp.bfloat16),
            pltpu.VMEM((NZ, 2, 2 * DEPTH, WIDTH), jnp.float32),
            pltpu.VMEM((NZ, NY * NC * TILES, 2, 8, WIDTH), jnp.float32),
            dma,
            dma((1,)),
            dma((1,)),
            dma((2, 3)),
            dma((2, 3)),
            dma((4,)),
            dma((4,)),
            dma((3,)),
            dma((3,)),
            dma((3,)),
            dma((3,)),
            dma((4, 4)),
            dma((4, 4)),
            dma((3, 4)),
            dma((3, 4)),
            dma((7, 3)),
            dma((7, 3)),
            dma((9, 7)),
            dma((9, 7)),
            pltpu.VMEM((len(MIRRORED), WIDTH, 6 * OWN), jnp.float32),
            pltpu.VMEM((len(MIRRORED), 2, OWN, 6 * OWN), jnp.float32),
            dma((len(MIRRORED), 2)),
            dma((len(MIRRORED), 2)),
        ],
        compiler_params=pltpu.CompilerParams(
            collective_id=0, has_side_effects=True, vmem_limit_bytes=48 * 2**20
        ),
    )(pltpu.with_memory_space_constraint(jacobian, pltpu.HBM))
    tiles = tiles.reshape(TILES, NY * NZ * 2 * NC, 8, WIDTH)
    return jnp.transpose(tiles, (0, 2, 1, 3)).reshape(OWN, NY * NZ * 2 * NC * WIDTH)


def solution(mesh):
    return jax.shard_map(
        per_device,
        mesh=mesh,
        in_specs=(P("grp", "loop"),),
        out_specs=P(("loop", "grp"), None),
        check_vma=False,
    )
```
